128 devices in a mesh: front: 4 (over z), blk: 32 (over x, y, core).
Axes of the slice: x: 4, y: 4, z: 4, core: 2. Of those that a mesh axis runs over, the one named last changes fastest.
Arguments:
- panel_column: bfloat16 [4, 16384, 256], P('front', 'blk'), may hold values from -6 to 6
- upper_inverse: bfloat16 [4, 256, 256], P('front'), may hold values from -0.375 to 0.375
- panel_rows: bfloat16 [4, 256, 12288], P('front', None, 'blk'), may hold values from -0.375 to 0.375
- trailing: bfloat16 [4, 16384, 12288], P('front', 'blk')
- sketch: bfloat16 [12288, 256], replicated, may hold values from -0.0546875 to 0.0546875
- row_map: int32 [4, 64, 256], P('front', 'blk'), may hold values from 0 to 255, each once within a row
- parent_block: int32 [4, 64], replicated, may hold values from 0 to 95, as said below
- parent_slot: int32 [96], replicated, may hold values from 0 to 127, as said below
Outputs:
- factored_column: bfloat16 [4, 16384, 256], P('front', 'blk')
- right_factor: bfloat16 [4, 12288, 256], P('front', 'blk')
- parent_left: bfloat16 [32768, 1024], P(('front', 'blk'))
The draws below stay inside these ranges and needn't reach their ends.
Inputs may be any that keep to these rules, and one draw needn't show every extreme that they name: `parent_block`: within one front the 64 blocks go to distinct parent blocks; some parent block receives a block of every front. `parent_slot`: distinct values: a device owns at most one parent block.
All inputs are finite; a program needn't handle non-finite values.
Results may differ from the reference program's by a relative error of at most 0.0095.
Values may be sent and summed in bfloat16 or wider, within the bound.
A program may use at most 128 MiB of HBM per device.

```python
import math
import jax
import jax.numpy as jnp
from jax import lax

BLOCK = 256
PANEL = 256
RANK = 256
COLS = 12288
FRONTS = 4
SLAB = 16384
NB = 64
PBLOCKS = 96
N_FRONT = 4
N_BLK = 32


def draw_trailing(key, part):
    seed_key = jax.random.fold_in(key, 11)
    entry_key, row_key, col_key = jax.random.split(seed_key, 3)
    shape = (FRONTS, SLAB, COLS)
    entries = jax.random.normal(entry_key, shape, jnp.float32)
    growth = 3.0
    position = jnp.arange(SLAB, dtype=jnp.float32) / SLAB
    row_scale = 10.0 ** jax.random.uniform(row_key, (FRONTS, SLAB, 1), jnp.float32, -0.5, 0.5)
    row_scale = row_scale * growth ** (position[None, :, None] - 0.5)
    col_scale = 10.0 ** jax.random.uniform(col_key, (1, 1, COLS), jnp.float32, -0.5, 0.5)
    return (entries * row_scale * col_scale).astype(jnp.bfloat16)


def draw_parent_block(key, part):
    seed_key = jax.random.fold_in(key, 23)

    def pick_front(front_number):
        front_key = jax.random.fold_in(seed_key, front_number)
        first_key, second_key = jax.random.split(front_key)
        others = jax.random.permutation(first_key, PBLOCKS - 1)[:NB - 1].astype(jnp.int32) + 1
        chosen = jnp.concatenate([jnp.zeros((1,), jnp.int32), others])
        return jax.random.permutation(second_key, chosen)
    return jax.vmap(pick_front)(jnp.arange(FRONTS, dtype=jnp.int32)).astype(jnp.int32)


def draw_parent_slot(key, part):
    seed_key = jax.random.fold_in(key, 37)
    return jax.random.permutation(seed_key, N_FRONT * N_BLK)[:PBLOCKS].astype(jnp.int32)


def block_levels(own_key, shape, cuts, smallest, high):
    def one(axis_at, blocks):
        draws = jax.random.uniform(jax.random.fold_in(jax.random.fold_in(own_key, 6), axis_at), (blocks,), jnp.float32, smallest / len(cuts), high / len(cuts))
        return jnp.repeat(jnp.exp(draws), shape[axis_at] // blocks).reshape((-1,) + (1,) * (len(shape) - axis_at - 1))

    loudness = one(*cuts[0])
    for cut in cuts[1:]:
        loudness = loudness * one(*cut)
    return loudness


def gaussian(rng, extent, spread, most, shards=(), held_as=jnp.bfloat16):
    factor_of = block_levels(rng, extent, shards, -0.22, 0.18) if shards else 1.0
    values = jax.random.normal(rng, extent, jnp.float32) * spread * factor_of
    return jnp.minimum(jnp.maximum(values, -most), most).astype(held_as)


def setup_inputs(seed: int = 0) -> dict:
    streams_of = jax.random.split(jax.random.key(seed), 9)
    panel_column = gaussian(streams_of[0], (FRONTS, SLAB, PANEL), 1.0, 6.0, ((0, 4), (1, 32)))
    upper_inverse = gaussian(streams_of[1], (FRONTS, PANEL, PANEL), PANEL ** -0.5, 0.375, ((0, 4),))
    panel_rows = gaussian(streams_of[2], (FRONTS, PANEL, COLS), PANEL ** -0.5, 0.375, ((0, 4), (2, 32)))
    trailing = draw_trailing(jax.random.fold_in(streams_of[8], 71), 0)
    sketch = gaussian(streams_of[4], (COLS, RANK), COLS ** -0.5, 0.0546875)
    row_map = jax.vmap(lambda own: jax.random.permutation(own, BLOCK))(jax.random.split(streams_of[5], FRONTS * NB)).reshape((FRONTS, NB, BLOCK)).astype(jnp.int32)
    parent_block = draw_parent_block(jax.random.fold_in(streams_of[8], 71), 0)
    parent_slot = draw_parent_slot(jax.random.fold_in(streams_of[8], 71), 0)
    return {"panel_column": panel_column, "upper_inverse": upper_inverse, "panel_rows": panel_rows, "trailing": trailing, "sketch": sketch, "row_map": row_map, "parent_block": parent_block, "parent_slot": parent_slot}


def reference(panel_column, upper_inverse, panel_rows, trailing, sketch, row_map, parent_block, parent_slot):
    global_sketch = sketch

    def per_front(operands):
        column, inverse, pivot_rows, trail = operands
        factored = jnp.dot(column.astype(jnp.float32), inverse.astype(jnp.float32), preferred_element_type=jnp.float32).astype(jnp.bfloat16)
        updated = (trail.astype(jnp.float32) - jnp.dot(factored.astype(jnp.float32), pivot_rows.astype(jnp.float32), preferred_element_type=jnp.float32)).astype(jnp.bfloat16)
        sketched = jnp.dot(updated.astype(jnp.float32), global_sketch.astype(jnp.float32), preferred_element_type=jnp.float32).astype(jnp.bfloat16)
        gram_matrix = jnp.dot(sketched.T.astype(jnp.float32), sketched.astype(jnp.float32), preferred_element_type=jnp.float32) / SLAB
        factor_low = jnp.linalg.cholesky(gram_matrix)
        basis_rows = jax.scipy.linalg.solve_triangular(factor_low, sketched.astype(jnp.float32).T, lower=True).T
        cross_terms = jnp.dot(updated.T.astype(jnp.float32), sketched.astype(jnp.float32), preferred_element_type=jnp.float32)
        right_rows = jax.scipy.linalg.solve_triangular(factor_low, cross_terms.T, lower=True).T / math.sqrt(SLAB)
        return (factored, right_rows.astype(jnp.bfloat16), basis_rows.astype(jnp.bfloat16))
    factored_column, right_factor, left_factor = lax.map(per_front, (panel_column, upper_inverse, panel_rows, trailing))
    owner_index = parent_slot[parent_block]
    row_target = (owner_index[:, :, None] * BLOCK + row_map).reshape(FRONTS, SLAB).astype(jnp.int32)
    front_column = jnp.broadcast_to(jnp.arange(FRONTS, dtype=jnp.int32)[:, None], (FRONTS, SLAB))
    parent_rows = jnp.zeros((N_FRONT * N_BLK * BLOCK, FRONTS, RANK), left_factor.dtype)
    parent_rows = parent_rows.at[row_target, front_column].set(left_factor)
    parent_left = parent_rows.reshape(N_FRONT * N_BLK * BLOCK, FRONTS * RANK)
    return (factored_column, right_factor, parent_left)
```

```python
import math

import jax
import jax.numpy as jnp
from jax import lax
from jax.experimental import pallas as pl
from jax.experimental.pallas import tpu as pltpu
from jax.sharding import PartitionSpec as P

F32 = jnp.float32
BF16 = jnp.bfloat16
MESH = pl.DeviceIdType.MESH
VLIM = 62 * 1024 * 1024

ORDER = (
    (2, 2), (2, 0), (2, 1), (2, 3), (0, 2), (1, 2), (3, 2), (1, 1),
    (3, 3), (1, 3), (3, 1), (1, 0), (0, 1), (3, 0), (0, 3), (0, 0),
)


def dot(a, b):
    return jnp.dot(a, b, preferred_element_type=F32)


def split(a):
    high = a.astype(BF16)
    return high, (a - high.astype(F32)).astype(BF16)


def remote(src, dst, send_sem, recv_sem, where):
    return pltpu.make_async_remote_copy(
        src_ref=src,
        dst_ref=dst,
        send_sem=send_sem,
        recv_sem=recv_sem,
        device_id=where,
        device_id_type=MESH,
    )


def await_bytes(ref, sem):
    pltpu.make_async_copy(ref, ref, sem).wait()


def panel_kernel(
    col_ref, uinv_ref, prow_ref, t_hbm, om_hbm,
    l_out, s_out, gm_out, x_out,
    t_v, om_v, own_v, y_v, st_v,
    q_send, q_recv, q_bc, q_full, gm_send, gm_recv, gm_bc, gm_full,
    pair_s, pair_r, s1_s, s1_r, acc, s2_s, s2_r, s3_s, s3_r,
    ld_sem, ar_ss, ar_rs, pair_ss, pair_rs, s1_ss, s1_rs, s2_ss, s2_rs, s3_ss, s3_rs,
):
    me = lax.axis_index("blk")
    n = 32
    x, y, c = me // 8, (me // 2) % 4, me % 2
    cols = t_v.shape[1]
    wide = cols // n
    loads = 8
    step = cols // loads

    own_copy = pltpu.make_async_copy(
        om_hbm.at[pl.ds(pl.multiple_of(me * wide, wide), wide)], own_v, ld_sem.at[loads]
    )
    own_copy.start()
    copies = []
    for k in range(loads):
        part = pl.ds(k * step, step)
        pair = (
            pltpu.make_async_copy(om_hbm.at[part], om_v.at[part], ld_sem.at[loads + 1 + k]),
            pltpu.make_async_copy(t_hbm.at[:, part], t_v.at[:, part], ld_sem.at[k]),
        )
        for one in pair:
            one.start()
        copies.append(pair)

    barrier = pltpu.get_barrier_semaphore()

    @pl.loop(1, n)
    def _(i):
        pl.semaphore_signal(
            barrier, inc=1, device_id={"blk": lax.rem(me + i, n)}, device_id_type=MESH
        )

    def scatter(src, dst, phase):
        @pl.loop(1, n)
        def _(i):
            peer = lax.rem(me + i, n)
            remote(
                src.at[peer], dst.at[i], ar_ss.at[phase], ar_rs.at[phase], {"blk": peer}
            ).start()

    def spread(src, dst, phase):
        @pl.loop(1, n)
        def _(i):
            peer = lax.rem(me + i, n)
            remote(src, dst.at[me], ar_ss.at[phase], ar_rs.at[phase], {"blk": peer}).start()

    def all_came(dst, phase):
        await_bytes(dst.at[pl.ds(1, n - 1)], ar_rs.at[phase])

    own_copy.wait()
    q_send[...] = dot(prow_ref[...], own_v[...]).reshape(q_send.shape)
    factored = dot(col_ref[...], uinv_ref[...]).astype(BF16)
    l_out[...] = factored
    pl.semaphore_wait(barrier, n - 1)
    scatter(q_send, q_recv, 0)
    q_recv[0] = q_send[me]

    def sketch_step(k):
        for one in copies[k]:
            one.wait()
        part = pl.ds(k * step, step)
        out = dot(t_v[:, part], om_v[part, :])
        if k == 0:
            y_v[...] = out
        else:
            y_v[...] += out

    for k in range(loads // 2):
        sketch_step(k)
    all_came(q_recv, 0)
    total = jnp.sum(q_recv[...], axis=0)
    q_bc[...] = total
    q_full[me] = total
    spread(q_bc, q_full, 1)
    for k in range(loads // 2, loads):
        sketch_step(k)
    all_came(q_full, 1)
    q_high, q_low = split(q_full[...].reshape(256, 256))
    sk32 = y_v[...] - dot(factored, q_high) - dot(factored, q_low)
    sk = sk32.astype(BF16)
    s_out[...] = sk
    st_v[...] = sk32.T.astype(BF16)
    st = st_v[...]
    gram = dot(st, sk).reshape(n, 8, 256)
    mix = dot(st, factored).reshape(n, 8, 256)
    gm_send[...] = jnp.concatenate([gram, mix], axis=1).astype(BF16)
    scatter(gm_send, gm_recv, 2)
    gm_recv[0] = gm_send[me]

    def chip(dx, dy):
        return lax.rem(x + dx, 4) * 4 + lax.rem(y + dy, 4)

    def place(dx, dy):
        return {"blk": chip(dx, dy) * 2 + c}

    def chunk(owner):
        return dot(st_v[...], t_v[:, pl.ds(pl.multiple_of(owner * wide, 128), wide)])

    waits = []

    def send(src, dst, ss, rs, where):
        copy = remote(src, dst, ss, rs, where)
        copy.start()
        waits.append(copy)
        return copy

    partner = {"blk": chip(0, 0) * 2 + (1 - c)}
    pairs = []
    for i, (dx, dy) in enumerate(ORDER):
        pair_s[i] = chunk(chip(dx, dy) * 2 + (1 - c)).astype(BF16)
        pairs.append(send(pair_s.at[i], pair_r.at[i], pair_ss.at[i], pair_rs.at[i], partner))
        if i == 11:
            all_came(gm_recv, 2)
            total = jnp.sum(gm_recv[...].astype(F32), axis=0)
            gm_bc[...] = total
            gm_full[me] = total
            spread(gm_bc, gm_full, 3)

    first = {}
    towards = (
        (lambda d: place(d, 0), lambda d: place(0, d)),
        (lambda d: place(0, d), lambda d: place(d, 0)),
    )

    def handle(h, d1, d2, v):
        go = towards[h][0]
        if d1 == 0:
            acc[h, d2] = v
            return
        if d1 == 2:
            slot, where = d2, go(1) if d2 < 2 else go(3)
        else:
            if (d2 < 2) == (d1 == 1):
                first[h, d2].wait_recv()
                v = v + s1_r[h, d2].astype(F32)
            slot, where = (4 + d2, go(1)) if d1 == 1 else (8 + d2, go(3))
        s1_s[h, slot] = v.astype(BF16)
        first[h, slot] = send(
            s1_s.at[h, slot], s1_r.at[h, slot], s1_ss.at[h, slot], s1_rs.at[h, slot], where
        )

    for i, (dx, dy) in enumerate(ORDER):
        v = chunk(chip(dx, dy) * 2 + c)
        pairs[i].wait_recv()
        v = v + pair_r[i].astype(F32)
        handle(0, dx, dy, v[:128])
        handle(1, dy, dx, v[128:])

    half, full = {}, {}
    for d2 in (2, 1, 3, 0):
        for h in range(2):
            go = towards[h][1]
            first[h, 4 + d2].wait_recv()
            first[h, 8 + d2].wait_recv()
            v = acc[h, d2] + s1_r[h, 4 + d2].astype(F32) + s1_r[h, 8 + d2].astype(F32)
            if d2 == 2:
                for k in range(2):
                    s2_s[h, k] = v[64 * k : 64 * k + 64].astype(BF16)
                    half[h, k] = send(
                        s2_s.at[h, k], s2_r.at[h, k], s2_ss.at[h, k], s2_rs.at[h, k], go(1 + 2 * k)
                    )
            elif d2 == 0:
                for k in range(2):
                    full[h, k].wait_recv()
                    v = v + s3_r[h, k].astype(F32)
                x_out[h * 128 : h * 128 + 128, :] = v
            else:
                k = d2 // 2
                half[h, k].wait_recv()
                more = s2_r[h, k].astype(F32)
                low, high = v[:64], v[64:]
                if k == 0:
                    low = low + more
                else:
                    high = high + more
                s3_s[h, k, 0:64, :] = low.astype(BF16)
                s3_s[h, k, 64:128, :] = high.astype(BF16)
                full[h, k] = send(
                    s3_s.at[h, k], s3_r.at[h, k], s3_ss.at[h, k], s3_rs.at[h, k], go(d2)
                )
    all_came(gm_full, 3)
    gm_out[...] = gm_full[...]
    for copy in waits:
        copy.wait_send()
    await_bytes(q_send.at[pl.ds(1, n - 1)], ar_ss.at[0])
    await_bytes(q_full.at[pl.ds(1, n - 1)], ar_ss.at[1])
    await_bytes(gm_send.at[pl.ds(1, n - 1)], ar_ss.at[2])
    await_bytes(gm_full.at[pl.ds(1, n - 1)], ar_ss.at[3])


def panel_call(column, inverse, rows, trailing, sketch):
    length, cols = trailing.shape
    wide = rows.shape[1]
    vmem = pl.BlockSpec(memory_space=pltpu.VMEM)
    anyw = pl.BlockSpec(memory_space=pl.ANY)
    dma = pltpu.SemaphoreType.DMA
    return pl.pallas_call(
        panel_kernel,
        out_shape=(
            jax.ShapeDtypeStruct((length, 256), BF16),
            jax.ShapeDtypeStruct((length, 256), BF16),
            jax.ShapeDtypeStruct((32, 16, 256), F32),
            jax.ShapeDtypeStruct((256, wide), F32),
        ),
        in_specs=[vmem, vmem, vmem, anyw, anyw],
        out_specs=(vmem, vmem, vmem, vmem),
        scratch_shapes=[
            pltpu.VMEM((length, cols), BF16),
            pltpu.VMEM((cols, 256), BF16),
            pltpu.VMEM((wide, 256), BF16),
            pltpu.VMEM((length, 256), F32),
            pltpu.VMEM((256, length), BF16),
            pltpu.VMEM((32, 8, 256), F32),
            pltpu.VMEM((32, 8, 256), F32),
            pltpu.VMEM((8, 256), F32),
            pltpu.VMEM((32, 8, 256), F32),
            pltpu.VMEM((32, 16, 256), BF16),
            pltpu.VMEM((32, 16, 256), BF16),
            pltpu.VMEM((16, 256), F32),
            pltpu.VMEM((32, 16, 256), F32),
            pltpu.VMEM((16, 256, wide), BF16),
            pltpu.VMEM((16, 256, wide), BF16),
            pltpu.VMEM((2, 12, 128, wide), BF16),
            pltpu.VMEM((2, 12, 128, wide), BF16),
            pltpu.VMEM((2, 4, 128, wide), F32),
            pltpu.VMEM((2, 2, 64, wide), BF16),
            pltpu.VMEM((2, 2, 64, wide), BF16),
            pltpu.VMEM((2, 2, 128, wide), BF16),
            pltpu.VMEM((2, 2, 128, wide), BF16),
            dma((17,)),
            dma((4,)),
            dma((4,)),
            dma((16,)),
            dma((16,)),
            dma((2, 12)),
            dma((2, 12)),
            dma((2, 2)),
            dma((2, 2)),
            dma((2, 2)),
            dma((2, 2)),
        ],
        compiler_params=pltpu.CompilerParams(
            collective_id=0, has_side_effects=True, vmem_limit_bytes=VLIM
        ),
        name="panel",
    )(column, inverse, rows, trailing, sketch)


def inverse_factor(a_ref, block=64):
    size = a_ref.shape[0]
    lane = lax.broadcasted_iota(jnp.int32, (8, size), 1)
    sub = lax.broadcasted_iota(jnp.int32, (8, 1), 0)
    for k in range(size // block):
        base = k * block
        tiles = [a_ref[base + 8 * t : base + 8 * t + 8, :] for t in range(block // 8)]
        pivots = [jnp.ones((8, 1), F32) for _ in tiles]
        for j in range(block):
            at, row = base + j, j % 8
            here = lane == at
            mine = tiles[j // 8]
            pivot_row = mine[row : row + 1, :]
            pivot = pivot_row[:, at : at + 1]
            scaled = jnp.where(here[:1], 1.0, pivot_row) * (1.0 / pivot)
            pivots[j // 8] = jnp.where(sub == row, pivot, pivots[j // 8])
            for t in range(j // 8, block // 8):
                tile = tiles[t]
                factor = tile[:, at : at + 1]
                if t == j // 8:
                    below = sub > row
                    factor = jnp.where(below, factor, 0.0)
                    kept = jnp.where(here, jnp.where(sub == row, 1.0, jnp.where(below, 0.0, tile)), tile)
                else:
                    kept = jnp.where(here, 0.0, tile)
                tiles[t] = kept - factor * scaled
        rest = base + block
        for t in range(block // 8):
            stale = (lane > sub + (base + 8 * t)) & (lane < rest)
            tile = jnp.where(stale, 0.0, tiles[t] * lax.rsqrt(pivots[t]))
            a_ref[base + 8 * t : base + 8 * t + 8, :] = tile
        if rest < size:
            done = a_ref[base:rest, :]
            change = lax.dot_general(
                done[:, rest:],
                done,
                (((0,), (0,)), ((), ())),
                precision=lax.Precision.HIGHEST,
                preferred_element_type=F32,
            )
            column = lax.broadcasted_iota(jnp.int32, (size - rest, size), 1)
            inside = (column >= base) & (column < rest)
            a_ref[rest:, :] = jnp.where(inside, 0.0, a_ref[rest:, :]) - change


def factor_kernel(slab_rows, s_ref, gm_ref, x_ref, prow_ref, map_ref, right_ref, left_ref, a_ref):
    size = 256
    a_ref[...] = gm_ref[:, :8, :].reshape(size, size) * (1.0 / slab_rows)
    inverse_factor(a_ref)
    row = lax.broadcasted_iota(jnp.int32, (size, size), 0)
    column = lax.broadcasted_iota(jnp.int32, (size, size), 1)
    w = jnp.where(column <= row, a_ref[...], 0.0)
    mix_high, mix_low = split(gm_ref[:, 8:, :].reshape(size, size))
    cross = x_ref[...] - dot(mix_high, prow_ref[...]) - dot(mix_low, prow_ref[...])
    w_high, w_low = split(w)
    c_high, c_low = split(cross)
    right = dot(w_high, c_high) + dot(w_high, c_low) + dot(w_low, c_high)
    right_ref[...] = (right.T * (1.0 / math.sqrt(slab_rows))).astype(BF16)
    turn = (((1,), (1,)), ((), ()))
    sk = s_ref[...]
    left = lax.dot_general(sk, w_high, turn, preferred_element_type=F32)
    left = (left + lax.dot_general(sk, w_low, turn, preferred_element_type=F32)).astype(BF16)
    for k in range(2):
        pick = (map_ref[k : k + 1, :] == row).astype(BF16)
        left_ref[k] = dot(pick, left[k * size : k * size + size]).astype(BF16)


def factor_call(slab_rows, sk, gm, xt, rows, row_map):
    wide = rows.shape[1]
    vmem = pl.BlockSpec(memory_space=pltpu.VMEM)

    def body(*refs):
        factor_kernel(slab_rows, *refs)

    return pl.pallas_call(
        body,
        out_shape=(
            jax.ShapeDtypeStruct((wide, 256), BF16),
            jax.ShapeDtypeStruct((2, 256, 256), BF16),
        ),
        in_specs=[vmem] * 5,
        out_specs=(vmem, vmem),
        scratch_shapes=[pltpu.VMEM((256, 256), F32)],
        compiler_params=pltpu.CompilerParams(vmem_limit_bytes=32 * 1024 * 1024),
        name="factor",
    )(sk, gm, xt, rows, row_map)


def place_kernel(table, in_ref, out_ref, buf_a, stage, buf_b, buf_c, a_ss, a_rs, b_ss, b_rs, c_ss, c_rs):
    me = lax.axis_index("blk")
    front = lax.axis_index("front")
    n, fronts = 32, 4
    barrier = pltpu.get_barrier_semaphore()

    @pl.loop(1, n)
    def _(i):
        pl.semaphore_signal(
            barrier, inc=1, device_id={"blk": lax.rem(me + i, n)}, device_id_type=MESH
        )

    for i in range(1, fronts):
        pl.semaphore_signal(
            barrier, inc=1, device_id={"front": lax.rem(front + i, fronts)}, device_id_type=MESH
        )
    pl.semaphore_wait(barrier, n - 1 + fronts - 1)

    @pl.loop(1, n)
    def _(i):
        peer = lax.rem(me + i, n)
        remote(in_ref.at[peer], buf_a.at[me], a_ss, a_rs, {"blk": peer}).start()

    buf_a[me] = in_ref[me]
    buf_a[n] = jnp.zeros(buf_a.shape[1:], BF16)
    await_bytes(buf_a.at[pl.ds(0, n - 1)], a_rs)

    def choose(g):
        @pl.loop(0, n)
        def _(t):
            j = table[g * n + t]
            stage[g, t] = buf_a[j // 2, lax.rem(j, 2)]

    sends = []
    for i in range(1, fronts):
        g = lax.rem(front + i, fronts)
        choose(g)
        copy = remote(stage.at[g], buf_b.at[front], b_ss.at[i], b_rs.at[i], {"front": g})
        copy.start()
        sends.append(copy)
    choose(front)
    buf_b[front] = stage[front]
    for copy in sends:
        copy.wait_recv()

    @pl.loop(1, n)
    def _(i):
        peer = lax.rem(me + i, n)
        remote(buf_b.at[:, peer], buf_c.at[me], c_ss, c_rs, {"blk": peer}).start()

    buf_c[me] = buf_b[:, me]
    await_bytes(buf_c.at[pl.ds(0, n - 1)], c_rs)
    out_ref[...] = buf_c[...]
    for copy in sends:
        copy.wait_send()
    await_bytes(in_ref.at[pl.ds(0, n - 1)], a_ss)
    await_bytes(buf_c.at[pl.ds(0, n - 1)], c_ss)


def place_call(table, pieces):
    vmem = pl.BlockSpec(memory_space=pltpu.VMEM)
    dma = pltpu.SemaphoreType.DMA
    return pl.pallas_call(
        place_kernel,
        out_shape=jax.ShapeDtypeStruct((32, 4, 16, 128), BF16),
        in_specs=[pl.BlockSpec(memory_space=pltpu.SMEM), vmem],
        out_specs=vmem,
        scratch_shapes=[
            pltpu.VMEM((33, 2, 16, 128), BF16),
            pltpu.VMEM((4, 32, 16, 128), BF16),
            pltpu.VMEM((4, 32, 16, 128), BF16),
            pltpu.VMEM((32, 4, 16, 128), BF16),
            dma(()),
            dma(()),
            dma((4,)),
            dma((4,)),
            dma(()),
            dma(()),
        ],
        compiler_params=pltpu.CompilerParams(
            collective_id=1, has_side_effects=True, vmem_limit_bytes=32 * 1024 * 1024
        ),
        name="place",
    )(table, pieces)


def body(
    panel_column, upper_inverse, panel_rows, trailing, sketch, row_map, parent_block, parent_slot
):
    slab_rows = trailing.shape[1] * lax.axis_size("blk")
    front = lax.axis_index("front")
    factored, sk, gm, xt = panel_call(
        panel_column[0], upper_inverse[0], panel_rows[0], trailing[0], sketch
    )
    blocks = lax.dynamic_slice(parent_block, (front, 0), (1, parent_block.shape[1]))[0]
    parents = jnp.arange(parent_slot.shape[0], dtype=jnp.int32)
    owners = jnp.sum(jnp.where(blocks[:, None] == parents[None, :], parent_slot[None, :], 0), axis=1)
    device = jnp.arange(128, dtype=jnp.int32)
    number = jnp.arange(blocks.shape[0], dtype=jnp.int32)
    table = 64 + jnp.sum(
        jnp.where(owners[None, :] == device[:, None], number[None, :] - 64, 0), axis=1
    )
    right, left = factor_call(slab_rows, sk, gm, xt, panel_rows[0], row_map[0])
    pieces = left.reshape(2, 32, 8, 2, 128).transpose(1, 0, 3, 2, 4).reshape(32, 2, 16, 128)
    placed = place_call(table, pieces)
    parent = placed.reshape(32, 4, 2, 8, 128).transpose(0, 3, 1, 2, 4).reshape(256, 1024)
    return factored[None], right[None], parent


def solution(mesh):
    return jax.shard_map(
        body,
        mesh=mesh,
        in_specs=(
            P("front", "blk", None),
            P("front", None, None),
            P("front", None, "blk"),
            P("front", "blk", None),
            P(),
            P("front", "blk", None),
            P(),
            P(),
        ),
        out_specs=(P("front", "blk", None), P("front", "blk", None), P(("front", "blk"), None)),
        check_vma=False,
    )
```

```python
import math

import jax
import jax.numpy as jnp
from jax import lax
from jax.experimental import pallas as pl
from jax.experimental.pallas import tpu as pltpu
from jax.sharding import PartitionSpec as P

F32 = jnp.float32
BF16 = jnp.bfloat16
MESH = pl.DeviceIdType.MESH
VLIM = 62 * 1024 * 1024

ORDER = (
    (2, 2), (2, 0), (2, 1), (2, 3), (0, 2), (1, 2), (3, 2), (1, 1),
    (3, 3), (1, 3), (3, 1), (1, 0), (0, 1), (3, 0), (0, 3), (0, 0),
)


def dot(a, b):
    return jnp.dot(a, b, preferred_element_type=F32)


def split(a):
    high = a.astype(BF16)
    return high, (a - high.astype(F32)).astype(BF16)


def remote(src, dst, send_sem, recv_sem, where):
    return pltpu.make_async_remote_copy(
        src_ref=src,
        dst_ref=dst,
        send_sem=send_sem,
        recv_sem=recv_sem,
        device_id=where,
        device_id_type=MESH,
    )


def await_bytes(ref, sem):
    pltpu.make_async_copy(ref, ref, sem).wait()


def factor_steps(a_ref, block=64, width=8, every=16):
    size = a_ref.shape[0]
    shape = (8, size)
    lane = lax.broadcasted_iota(jnp.int32, shape, 1)
    sub = lax.broadcasted_iota(jnp.int32, shape, 0)
    for k in range(size // block):
        base = k * block
        rest = base + block
        tiles = [a_ref[base + 8 * t : base + 8 * t + 8, :] for t in range(block // 8)]
        pivots = [jnp.ones(shape, F32) for _ in tiles]
        for j in range(0, block, width):
            at, low, own = base + j, j % 8, j // 8
            inside = (lane >= at) & (lane < at + width)

            def columns(tile):
                return [jnp.broadcast_to(tile[:, at + i : at + i + 1], shape) for i in range(width)]

            def line(tile, i):
                return jnp.broadcast_to(tile[low + i : low + i + 1, :], shape)

            mine = tiles[own]
            heads = columns(mine)
            m = [
                [line(heads[q], i) if q >= i else None for q in range(width)]
                for i in range(width)
            ]
            lines = [
                jnp.where(inside, jnp.where(lane == at + i, 1.0, 0.0), line(mine, i))
                for i in range(width)
            ]
            scales, mults = [], {}
            for i in range(width):
                inv = 1.0 / m[i][i]
                scales.append(inv)
                for q in range(i + 1, width):
                    mults[q, i] = m[i][q] * inv
                for q in range(i + 1, width):
                    for p in range(q, width):
                        m[q][p] = m[q][p] - mults[q, i] * m[i][p]
            for i in range(width):
                for q in range(i + 1, width):
                    lines[q] = lines[q] - mults[q, i] * lines[i]
            scaled = [lines[i] * scales[i] for i in range(width)]
            for t in range(own, block // 8):
                tile = tiles[t]
                cs = heads if t == own else columns(tile)
                cs = list(cs)
                for i in range(width):
                    for q in range(i + 1, width):
                        cs[q] = cs[q] - mults[q, i] * cs[i]
                out = jnp.where(inside, 0.0, tile)
                for i in range(width):
                    out = out - cs[i] * scaled[i]
                if t == own:
                    out = jnp.where(sub >= low + width, out, tile)
                    for i in range(width):
                        out = jnp.where(sub == low + i, lines[i], out)
                        pivots[t] = jnp.where(sub == low + i, m[i][i], pivots[t])
                tiles[t] = out
            if (j + width) % every == 0 and j + width < block:
                yield at + width
        for t in range(block // 8):
            stale = (lane > sub + (base + 8 * t)) & (lane < rest)
            tile = jnp.where(stale, 0.0, tiles[t] * lax.rsqrt(pivots[t]))
            a_ref[base + 8 * t : base + 8 * t + 8, :] = tile
        if rest < size:
            done = a_ref[base:rest, :]
            change = lax.dot_general(
                done[:, rest:],
                done,
                (((0,), (0,)), ((), ())),
                precision=lax.Precision.HIGHEST,
                preferred_element_type=F32,
            )
            column = lax.broadcasted_iota(jnp.int32, (size - rest, size), 1)
            within = (column >= base) & (column < rest)
            a_ref[rest:, :] = jnp.where(within, 0.0, a_ref[rest:, :]) - change
        yield rest


def fused_kernel(
    slab_rows,
    table, col_ref, uinv_ref, prow_ref, map_ref, t_hbm, om_hbm,
    l_out, right_out, z_out,
    t_v, om_v, own_v, y_v, st_v,
    q_send, q_recv, q_bc, q_full, gm_send, gm_recv, g_bc, g_full, m_bc, m_full,
    pair_s, pair_r, s1_s, s1_r, acc, s2_s, s2_r, s3_s, s3_r, x_v, a_ref,
    a0, a3, c1, c4, big, z_s, z_r,
    ld_sem, ar_ss, ar_rs, pair_ss, pair_rs, s1_ss, s1_rs, s2_ss, s2_rs, s3_ss, s3_rs,
    z_ss, z_rs,
):
    me = lax.axis_index("blk")
    front = lax.axis_index("front")
    n, fronts, size = 32, 4, 256
    x, y, c = me // 8, (me // 2) % 4, me % 2
    cols = t_v.shape[1]
    wide = cols // n
    loads = 8
    step = cols // loads

    barrier = pltpu.get_barrier_semaphore()

    @pl.loop(1, n)
    def _(i):
        pl.semaphore_signal(
            barrier, inc=1, device_id={"blk": lax.rem(me + i, n)}, device_id_type=MESH
        )

    for i in range(1, fronts):
        pl.semaphore_signal(
            barrier, inc=1, device_id={"front": lax.rem(front + i, fronts)}, device_id_type=MESH
        )

    own_copy = pltpu.make_async_copy(
        om_hbm.at[pl.ds(pl.multiple_of(me * wide, wide), wide)], own_v, ld_sem.at[loads]
    )
    own_copy.start()
    copies = []
    for k in range(loads):
        part = pl.ds(k * step, step)
        pair = (
            pltpu.make_async_copy(om_hbm.at[part], om_v.at[part], ld_sem.at[loads + 1 + k]),
            pltpu.make_async_copy(t_hbm.at[:, part], t_v.at[:, part], ld_sem.at[k]),
        )
        for one in pair:
            one.start()
        copies.append(pair)

    def scatter(src, dst, phase):
        @pl.loop(1, n)
        def _(i):
            peer = lax.rem(me + i, n)
            remote(
                src.at[peer], dst.at[i], ar_ss.at[phase], ar_rs.at[phase], {"blk": peer}
            ).start()

    def spread(src, dst, phase):
        @pl.loop(1, n)
        def _(i):
            peer = lax.rem(me + i, n)
            remote(src, dst.at[me], ar_ss.at[phase], ar_rs.at[phase], {"blk": peer}).start()

    def all_came(dst, phase):
        await_bytes(dst.at[pl.ds(1, n - 1)], ar_rs.at[phase])

    def chip(dx, dy):
        return lax.rem(x + dx, 4) * 4 + lax.rem(y + dy, 4)

    def place(dx, dy):
        return {"blk": chip(dx, dy) * 2 + c}

    partner = {"blk": chip(0, 0) * 2 + (1 - c)}
    waits = []

    def send(src, dst, ss, rs, where):
        copy = remote(src, dst, ss, rs, where)
        copy.start()
        waits.append(copy)
        return copy

    own_copy.wait()
    q_send[...] = dot(prow_ref[...], own_v[...]).reshape(q_send.shape)
    factored = dot(col_ref[...], uinv_ref[...]).astype(BF16)
    l_out[...] = factored
    pl.semaphore_wait(barrier, n - 1 + fronts - 1)
    scatter(q_send, q_recv, 0)
    q_recv[0] = q_send[me]

    def sketch_step(k):
        for one in copies[k]:
            one.wait()
        part = pl.ds(k * step, step)
        out = dot(t_v[:, part], om_v[part, :])
        if k == 0:
            y_v[...] = out
        else:
            y_v[...] += out

    for k in range(loads // 2):
        sketch_step(k)
    all_came(q_recv, 0)
    total = jnp.sum(q_recv[...], axis=0)
    q_bc[...] = total
    q_full[me] = total
    spread(q_bc, q_full, 1)
    for k in range(loads // 2, loads):
        sketch_step(k)
    all_came(q_full, 1)
    q_high, q_low = split(q_full[...].reshape(size, size))
    sk32 = y_v[...] - dot(factored, q_high) - dot(factored, q_low)
    sk = sk32.astype(BF16)
    st_v[...] = sk32.T.astype(BF16)
    st = st_v[...]
    gram = dot(st, sk).reshape(n, 8, size)
    mix = dot(st, factored).reshape(n, 8, size)
    gm_send[...] = jnp.concatenate([gram, mix], axis=1).astype(BF16)
    scatter(gm_send, gm_recv, 2)
    gm_recv[0] = gm_send[me]
    row = lax.broadcasted_iota(jnp.int32, (size, size), 0)
    for k in range(2):
        pick = (map_ref[k : k + 1, :] == row).astype(BF16)
        moved = dot(pick, sk[k * size : k * size + size]).astype(BF16)
        for h in range(2):
            a0[:, h, k] = moved[:, 128 * h : 128 * h + 128].reshape(16, 16, 128)

    @pl.loop(1, n)
    def _(i):
        peer = lax.rem(me + i, n)
        remote(
            a0.at[peer // 2, lax.rem(peer, 2)],
            a3.at[pl.ds(2 * me, 2)],
            ar_ss.at[5],
            ar_rs.at[5],
            {"blk": peer},
        ).start()

    a3[pl.ds(2 * me, 2)] = a0[me // 2, c]
    a3[2 * n] = jnp.zeros((16, 128), BF16)

    def choose():
        await_bytes(a3.at[pl.ds(0, 2 * n - 2)], ar_rs.at[5])

        @pl.loop(0, n)
        def _(t):
            for g in range(fronts):
                c1[t, g] = a3[table[t * fronts + g]]

        @pl.loop(1, n)
        def _(i):
            peer = lax.rem(me + i, n)
            remote(
                c1.at[peer], c4.at[me // 2, c], ar_ss.at[6], ar_rs.at[6], {"blk": peer}
            ).start()

        c4[me // 2, c] = c1[me]

    def assemble():
        await_bytes(c1.at[pl.ds(0, n - 1)], ar_rs.at[6])
        for g in range(fronts):
            for h in range(2):
                big[g * size : g * size + size, 128 * h : 128 * h + 128] = c4[:, h, g].reshape(
                    size, 128
                )

    def chunk(owner):
        return dot(st_v[...], t_v[:, pl.ds(pl.multiple_of(owner * wide, 128), wide)])

    first, half, full = {}, {}, {}
    towards = (
        (lambda d: place(d, 0), lambda d: place(0, d)),
        (lambda d: place(0, d), lambda d: place(d, 0)),
    )

    def handle(h, d1, d2, v):
        go = towards[h][0]
        if d1 == 0:
            acc[h, d2] = v
            return
        if d1 == 2:
            slot, where = d2, go(1) if d2 < 2 else go(3)
        else:
            if (d2 < 2) == (d1 == 1):
                first[h, d2].wait_recv()
                v = v + s1_r[h, d2].astype(F32)
            slot, where = (4 + d2, go(1)) if d1 == 1 else (8 + d2, go(3))
        s1_s[h, slot] = v.astype(BF16)
        first[h, slot] = send(
            s1_s.at[h, slot], s1_r.at[h, slot], s1_ss.at[h, slot], s1_rs.at[h, slot], where
        )

    pairs = []

    def theirs(i):
        dx, dy = ORDER[i]
        pair_s[i] = chunk(chip(dx, dy) * 2 + (1 - c)).astype(BF16)
        pairs.append(send(pair_s.at[i], pair_r.at[i], pair_ss.at[i], pair_rs.at[i], partner))

    def ours(i):
        dx, dy = ORDER[i]
        v = chunk(chip(dx, dy) * 2 + c)
        pairs[i].wait_recv()
        v = v + pair_r[i].astype(F32)
        handle(0, dx, dy, v[:128])
        handle(1, dy, dx, v[128:])

    def second(d2, h):
        go = towards[h][1]
        first[h, 4 + d2].wait_recv()
        first[h, 8 + d2].wait_recv()
        v = acc[h, d2] + s1_r[h, 4 + d2].astype(F32) + s1_r[h, 8 + d2].astype(F32)
        if d2 == 2:
            for k in range(2):
                s2_s[h, k] = v[64 * k : 64 * k + 64].astype(BF16)
                half[h, k] = send(
                    s2_s.at[h, k], s2_r.at[h, k], s2_ss.at[h, k], s2_rs.at[h, k], go(1 + 2 * k)
                )
        elif d2 == 0:
            for k in range(2):
                full[h, k].wait_recv()
                v = v + s3_r[h, k].astype(F32)
            x_v[h * 128 : h * 128 + 128, :] = v
        else:
            k = d2 // 2
            half[h, k].wait_recv()
            more = s2_r[h, k].astype(F32)
            low, high = v[:64], v[64:]
            if k == 0:
                low = low + more
            else:
                high = high + more
            s3_s[h, k, 0:64, :] = low.astype(BF16)
            s3_s[h, k, 64:128, :] = high.astype(BF16)
            full[h, k] = send(s3_s.at[h, k], s3_r.at[h, k], s3_ss.at[h, k], s3_rs.at[h, k], go(d2))

    turn = (((1,), (1,)), ((), ()))
    z_sends = []

    def leave(h):
        low, up = 128 * h, 128 * h + 128
        lane = lax.broadcasted_iota(jnp.int32, (128, size), 1)
        line = lax.broadcasted_iota(jnp.int32, (128, size), 0) + low
        w_high, w_low = split(jnp.where(lane <= line, a_ref[low:up, :], 0.0))
        left = lax.dot_general(big[...], w_high, turn, preferred_element_type=F32)
        left = left + lax.dot_general(big[...], w_low, turn, preferred_element_type=F32)
        z_s[h] = left.astype(BF16).reshape(fronts, size, 128)
        for i in (2, 1, 3):
            g = lax.rem(front + i, fronts)
            z_sends.append(
                send(z_s.at[h, g], z_r.at[h, front], z_ss.at[h, i], z_rs.at[h, i], {"front": g})
            )
        z_r[h, front] = z_s[h, front]

    for i in range(16):
        theirs(i)
        if i >= 12:
            ours(i - 12)
    all_came(gm_recv, 2)
    total = jnp.sum(gm_recv[...].astype(F32), axis=0)
    g_bc[...] = total[:8]
    m_bc[...] = total[8:]
    g_full[me] = total[:8]
    m_full[me] = total[8:]
    spread(g_bc, g_full, 3)
    for i in range(4, 7):
        ours(i)
    choose()
    for i in range(7, 9):
        ours(i)
    second(2, 0)
    second(2, 1)
    for i in range(9, 11):
        ours(i)
    all_came(g_full, 3)
    a_ref[...] = g_full[...].reshape(size, size) * (1.0 / slab_rows)
    between = {
        64: lambda: (ours(11), ours(12), second(1, 0), second(1, 1)),
        128: lambda: (ours(13), ours(14), second(3, 0), second(3, 1), spread(m_bc, m_full, 4)),
        192: lambda: (ours(15), assemble(), leave(0)),
    }
    for count in factor_steps(a_ref):
        if count in between:
            between[count]()
    leave(1)
    second(0, 0)
    second(0, 1)
    all_came(m_full, 4)
    mix_high, mix_low = split(m_full[...].reshape(size, size))
    prow = prow_ref[...]
    cross = x_v[...] - dot(mix_high, prow) - dot(mix_low, prow)
    column = lax.broadcasted_iota(jnp.int32, (size, size), 1)
    w_high, w_low = split(jnp.where(column <= row, a_ref[...], 0.0))
    c_high, c_low = split(cross)
    right = dot(w_high, c_high) + dot(w_high, c_low) + dot(w_low, c_high)
    right_out[...] = (right.T * (1.0 / math.sqrt(slab_rows))).astype(BF16)
    for copy in z_sends:
        copy.wait_recv()
    z_out[...] = z_r[...]
    for copy in waits:
        copy.wait_send()
    await_bytes(q_send.at[pl.ds(1, n - 1)], ar_ss.at[0])
    await_bytes(q_full.at[pl.ds(1, n - 1)], ar_ss.at[1])
    await_bytes(gm_send.at[pl.ds(1, n - 1)], ar_ss.at[2])
    await_bytes(g_full.at[pl.ds(1, n - 1)], ar_ss.at[3])
    await_bytes(m_full.at[pl.ds(1, n - 1)], ar_ss.at[4])
    await_bytes(a3.at[pl.ds(0, 2 * n - 2)], ar_ss.at[5])
    await_bytes(c1.at[pl.ds(0, n - 1)], ar_ss.at[6])


def fused_call(slab_rows, table, column, inverse, rows, row_map, trailing, sketch):
    length, cols = trailing.shape
    wide = rows.shape[1]
    vmem = pl.BlockSpec(memory_space=pltpu.VMEM)
    anyw = pl.BlockSpec(memory_space=pl.ANY)
    dma = pltpu.SemaphoreType.DMA

    def kernel(*refs):
        fused_kernel(slab_rows, *refs)

    return pl.pallas_call(
        kernel,
        out_shape=(
            jax.ShapeDtypeStruct((length, 256), BF16),
            jax.ShapeDtypeStruct((wide, 256), BF16),
            jax.ShapeDtypeStruct((2, 4, 256, 128), BF16),
        ),
        in_specs=[pl.BlockSpec(memory_space=pltpu.SMEM), vmem, vmem, vmem, vmem, anyw, anyw],
        out_specs=(vmem, vmem, vmem),
        scratch_shapes=[
            pltpu.VMEM((length, cols), BF16),
            pltpu.VMEM((cols, 256), BF16),
            pltpu.VMEM((wide, 256), BF16),
            pltpu.VMEM((length, 256), F32),
            pltpu.VMEM((256, length), BF16),
            pltpu.VMEM((32, 8, 256), F32),
            pltpu.VMEM((32, 8, 256), F32),
            pltpu.VMEM((8, 256), F32),
            pltpu.VMEM((32, 8, 256), F32),
            pltpu.VMEM((32, 16, 256), BF16),
            pltpu.VMEM((32, 16, 256), BF16),
            pltpu.VMEM((8, 256), F32),
            pltpu.VMEM((32, 8, 256), F32),
            pltpu.VMEM((8, 256), F32),
            pltpu.VMEM((32, 8, 256), F32),
            pltpu.VMEM((16, 256, wide), BF16),
            pltpu.VMEM((16, 256, wide), BF16),
            pltpu.VMEM((2, 12, 128, wide), BF16),
            pltpu.VMEM((2, 12, 128, wide), BF16),
            pltpu.VMEM((2, 4, 128, wide), F32),
            pltpu.VMEM((2, 2, 64, wide), BF16),
            pltpu.VMEM((2, 2, 64, wide), BF16),
            pltpu.VMEM((2, 2, 128, wide), BF16),
            pltpu.VMEM((2, 2, 128, wide), BF16),
            pltpu.VMEM((256, wide), F32),
            pltpu.VMEM((256, 256), F32),
            pltpu.VMEM((16, 2, 2, 16, 128), BF16),
            pltpu.VMEM((65, 16, 128), BF16),
            pltpu.VMEM((32, 4, 16, 128), BF16),
            pltpu.VMEM((16, 2, 4, 16, 128), BF16),
            pltpu.VMEM((1024, 256), BF16),
            pltpu.VMEM((2, 4, 256, 128), BF16),
            pltpu.VMEM((2, 4, 256, 128), BF16),
            dma((17,)),
            dma((7,)),
            dma((7,)),
            dma((16,)),
            dma((16,)),
            dma((2, 12)),
            dma((2, 12)),
            dma((2, 2)),
            dma((2, 2)),
            dma((2, 2)),
            dma((2, 2)),
            dma((2, 4)),
            dma((2, 4)),
        ],
        compiler_params=pltpu.CompilerParams(
            collective_id=0, has_side_effects=True, vmem_limit_bytes=VLIM
        ),
        name="fused",
    )(table, column, inverse, rows, row_map, trailing, sketch)


def write_kernel(l_ref, right_ref, z_ref, l_out, right_out, parent_out):
    l_out[...] = l_ref[...]
    right_out[...] = right_ref[...]
    for g in range(4):
        for h in range(2):
            at = g * 256 + 128 * h
            parent_out[:, at : at + 128] = z_ref[h, g]


def write_call(factored, right, parts):
    vmem = pl.BlockSpec(memory_space=pltpu.VMEM)
    return pl.pallas_call(
        write_kernel,
        out_shape=(
            jax.ShapeDtypeStruct(factored.shape, BF16),
            jax.ShapeDtypeStruct(right.shape, BF16),
            jax.ShapeDtypeStruct((256, 1024), BF16),
        ),
        in_specs=[vmem] * 3,
        out_specs=(vmem, vmem, vmem),
        name="write",
    )(factored, right, parts)


def slot_table(parent_block, parent_slot):
    front = lax.axis_index("front")
    blocks = lax.dynamic_slice(parent_block, (front, 0), (1, parent_block.shape[1]))[0]
    parents = jnp.arange(parent_slot.shape[0], dtype=jnp.int32)
    owners = jnp.sum(jnp.where(blocks[:, None] == parents[None, :], parent_slot[None, :], 0), axis=1)
    slot = jnp.arange(128, dtype=jnp.int32)
    device = slot % 4 * 32 + slot // 4
    j = jnp.arange(blocks.shape[0], dtype=jnp.int32)
    return 64 + jnp.sum(jnp.where(owners[None, :] == device[:, None], j[None, :] - 64, 0), axis=1)


def body(
    panel_column, upper_inverse, panel_rows, trailing, sketch, row_map, parent_block, parent_slot
):
    slab_rows = trailing.shape[1] * lax.axis_size("blk")
    results = fused_call(
        slab_rows,
        slot_table(parent_block, parent_slot),
        panel_column[0],
        upper_inverse[0],
        panel_rows[0],
        row_map[0],
        trailing[0],
        sketch,
    )
    factored, right, parent = write_call(*results)
    return factored[None], right[None], parent


def solution(mesh):
    return jax.shard_map(
        body,
        mesh=mesh,
        in_specs=(
            P("front", "blk", None),
            P("front", None, None),
            P("front", None, "blk"),
            P("front", "blk", None),
            P(),
            P("front", "blk", None),
            P(),
            P(),
        ),
        out_specs=(P("front", "blk", None), P("front", "blk", None), P(("front", "blk"), None)),
        check_vma=False,
    )
```

```python
import math

import jax
import jax.numpy as jnp
from jax import lax
from jax.experimental import pallas as pl
from jax.experimental.pallas import tpu as pltpu
from jax.sharding import PartitionSpec as P

F32 = jnp.float32
BF16 = jnp.bfloat16
MESH = pl.DeviceIdType.MESH
VLIM = 62 * 1024 * 1024

ORDER = (
    (2, 2), (2, 0), (0, 2), (2, 1), (1, 2), (2, 3), (3, 2), (1, 3),
    (3, 1), (3, 0), (0, 3), (1, 0), (0, 1), (1, 1), (3, 3), (0, 0),
)


def dot(a, b):
    return jnp.dot(a, b, preferred_element_type=F32)


def split(a):
    high = a.astype(BF16)
    return high, (a - high.astype(F32)).astype(BF16)


def remote(src, dst, send_sem, recv_sem, where):
    return pltpu.make_async_remote_copy(
        src_ref=src,
        dst_ref=dst,
        send_sem=send_sem,
        recv_sem=recv_sem,
        device_id=where,
        device_id_type=MESH,
    )


def await_bytes(ref, sem):
    pltpu.make_async_copy(ref, ref, sem).wait()


def factor_steps(a_ref, block=64, width=8, every=16):
    size = a_ref.shape[0]
    shape = (8, size)
    lane = lax.broadcasted_iota(jnp.int32, shape, 1)
    sub = lax.broadcasted_iota(jnp.int32, shape, 0)
    for k in range(size // block):
        base = k * block
        rest = base + block
        tiles = [a_ref[base + 8 * t : base + 8 * t + 8, :] for t in range(block // 8)]
        pivots = [jnp.ones(shape, F32) for _ in tiles]
        for j in range(0, block, width):
            at, low, own = base + j, j % 8, j // 8
            inside = (lane >= at) & (lane < at + width)

            def columns(tile):
                return [jnp.broadcast_to(tile[:, at + i : at + i + 1], shape) for i in range(width)]

            def line(tile, i):
                return jnp.broadcast_to(tile[low + i : low + i + 1, :], shape)

            mine = tiles[own]
            heads = columns(mine)
            m = [
                [line(heads[q], i) if q >= i else None for q in range(width)]
                for i in range(width)
            ]
            lines = [
                jnp.where(inside, jnp.where(lane == at + i, 1.0, 0.0), line(mine, i))
                for i in range(width)
            ]
            scales, mults = [], {}
            for i in range(width):
                inv = 1.0 / m[i][i]
                scales.append(inv)
                for q in range(i + 1, width):
                    mults[q, i] = m[i][q] * inv
                for q in range(i + 1, width):
                    for p in range(q, width):
                        m[q][p] = m[q][p] - mults[q, i] * m[i][p]
            for i in range(width):
                for q in range(i + 1, width):
                    lines[q] = lines[q] - mults[q, i] * lines[i]
            scaled = [lines[i] * scales[i] for i in range(width)]
            for t in range(own, block // 8):
                tile = tiles[t]
                cs = heads if t == own else columns(tile)
                cs = list(cs)
                for i in range(width):
                    for q in range(i + 1, width):
                        cs[q] = cs[q] - mults[q, i] * cs[i]
                out = jnp.where(inside, 0.0, tile)
                for i in range(width):
                    out = out - cs[i] * scaled[i]
                if t == own:
                    out = jnp.where(sub >= low + width, out, tile)
                    for i in range(width):
                        out = jnp.where(sub == low + i, lines[i], out)
                        pivots[t] = jnp.where(sub == low + i, m[i][i], pivots[t])
                tiles[t] = out
            if (j + width) % every == 0 and j + width < block:
                yield at + width
        for t in range(block // 8):
            stale = (lane > sub + (base + 8 * t)) & (lane < rest)
            tile = jnp.where(stale, 0.0, tiles[t] * lax.rsqrt(pivots[t]))
            a_ref[base + 8 * t : base + 8 * t + 8, :] = tile
        if rest < size:
            done = a_ref[base:rest, :]
            change = lax.dot_general(
                done[:, rest:],
                done,
                (((0,), (0,)), ((), ())),
                precision=lax.Precision.HIGHEST,
                preferred_element_type=F32,
            )
            column = lax.broadcasted_iota(jnp.int32, (size - rest, size), 1)
            within = (column >= base) & (column < rest)
            a_ref[rest:, :] = jnp.where(within, 0.0, a_ref[rest:, :]) - change
        yield rest


def fused_kernel(
    slab_rows,
    table, col_ref, uinv_ref, prow_ref, map_ref, t_hbm, om_hbm,
    l_out, right_out, z_out,
    t_v, om_v, own_v, y_v, st_v,
    q_send, q_pair, q_mid, q_recv, q_bc, q_full,
    gm_send, gm_pair, gm_mid, gm_recv, g_bc, g_full, m_bc, m_full,
    pair_s, pair_r, s1_s, s1_r, acc, s2_s, s2_r, s3_s, s3_r, x_v, a_ref,
    a0, a3, c1, c4, big, z_s, z_r,
    ld_sem, ar_ss, ar_rs, swap_ss, swap_rs, pair_ss, pair_rs, s1_ss, s1_rs, s2_ss, s2_rs, s3_ss, s3_rs,
    z_ss, z_rs,
):
    me = lax.axis_index("blk")
    front = lax.axis_index("front")
    n, fronts, size = 32, 4, 256
    x, y, c = me // 8, (me // 2) % 4, me % 2
    cols = t_v.shape[1]
    wide = cols // n
    loads = 8
    step = cols // loads

    barrier = pltpu.get_barrier_semaphore()

    @pl.loop(1, n)
    def _(i):
        pl.semaphore_signal(
            barrier, inc=1, device_id={"blk": lax.rem(me + i, n)}, device_id_type=MESH
        )

    for i in range(1, fronts):
        pl.semaphore_signal(
            barrier, inc=1, device_id={"front": lax.rem(front + i, fronts)}, device_id_type=MESH
        )

    own_copy = pltpu.make_async_copy(
        om_hbm.at[pl.ds(pl.multiple_of(me * wide, wide), wide)], own_v, ld_sem.at[loads]
    )
    own_copy.start()
    copies = []
    for k in range(loads):
        part = pl.ds(k * step, step)
        pair = (
            pltpu.make_async_copy(om_hbm.at[part], om_v.at[part], ld_sem.at[loads + 1 + k]),
            pltpu.make_async_copy(t_hbm.at[:, part], t_v.at[:, part], ld_sem.at[k]),
        )
        for one in pair:
            one.start()
        copies.append(pair)

    chips = n // 2
    mine = me // 2

    def scatter(src, dst, phase):
        @pl.loop(1, chips)
        def _(i):
            peer = lax.rem(mine + i, chips)
            remote(
                src.at[peer], dst.at[i], ar_ss.at[phase], ar_rs.at[phase], {"blk": peer * 2 + c}
            ).start()

        dst[0] = src[mine]

    def spread(src, dst, phase):
        @pl.loop(1, chips)
        def _(i):
            peer = lax.rem(mine + i, chips)
            remote(
                src, dst.at[c, mine], ar_ss.at[phase], ar_rs.at[phase], {"blk": peer * 2 + c}
            ).start()

        dst[c, mine] = src[...]

    def all_came(dst, phase):
        await_bytes(dst.at[pl.ds(1, chips - 1)], ar_rs.at[phase])

    def swap(i, src, dst):
        return send(src, dst, swap_ss.at[i], swap_rs.at[i], partner)

    def join(full, phase, i):
        await_bytes(full.at[0, pl.ds(1, chips - 1)], ar_rs.at[phase])
        return swap(i, full.at[c], full.at[c])

    def chip(dx, dy):
        return lax.rem(x + dx, 4) * 4 + lax.rem(y + dy, 4)

    def place(dx, dy):
        return {"blk": chip(dx, dy) * 2 + c}

    partner = {"blk": chip(0, 0) * 2 + (1 - c)}
    waits = []

    def send(src, dst, ss, rs, where):
        copy = remote(src, dst, ss, rs, where)
        copy.start()
        waits.append(copy)
        return copy

    own_copy.wait()
    q_send[...] = dot(prow_ref[...], own_v[...]).reshape(q_send.shape)
    factored = dot(col_ref[...], uinv_ref[...]).astype(BF16)
    l_out[...] = factored
    pl.semaphore_wait(barrier, n - 1 + fronts - 1)
    other = swap(0, q_send.at[1 - c], q_pair)

    def sketch_step(k):
        for one in copies[k]:
            one.wait()
        part = pl.ds(k * step, step)
        out = dot(t_v[:, part], om_v[part, :])
        if k == 0:
            y_v[...] = out
        else:
            y_v[...] += out

    sketch_step(0)
    other.wait_recv()
    q_mid[...] = q_send[c] + q_pair[...]
    scatter(q_mid, q_recv, 0)
    for k in range(1, 4):
        sketch_step(k)
    all_came(q_recv, 0)
    q_bc[...] = jnp.sum(q_recv[...], axis=0)
    spread(q_bc, q_full, 1)
    for k in range(4, loads):
        sketch_step(k)
    join(q_full, 1, 1).wait_recv()
    q_high, q_low = split(q_full[...].reshape(size, size))
    sk32 = y_v[...] - dot(factored, q_high) - dot(factored, q_low)
    sk = sk32.astype(BF16)
    st_v[...] = sk32.T.astype(BF16)
    st = st_v[...]
    gm_send[:, :, :8, :] = dot(st, sk).reshape(2, chips, 8, size)
    gm_send[:, :, 8:, :] = dot(st, factored).reshape(2, chips, 8, size)
    other = swap(2, gm_send.at[1 - c], gm_pair)
    row = lax.broadcasted_iota(jnp.int32, (size, size), 0)
    for k in range(2):
        pick = (map_ref[k : k + 1, :] == row).astype(BF16)
        moved = dot(pick, sk[k * size : k * size + size]).astype(BF16)
        for h in range(2):
            a0[:, h, k] = moved[:, 128 * h : 128 * h + 128].reshape(16, 16, 128)

    def spill():
        @pl.loop(1, n)
        def _(i):
            peer = lax.rem(me + i, n)
            remote(
                a0.at[peer // 2, lax.rem(peer, 2)],
                a3.at[pl.ds(2 * me, 2)],
                ar_ss.at[5],
                ar_rs.at[5],
                {"blk": peer},
            ).start()

    a3[pl.ds(2 * me, 2)] = a0[me // 2, c]
    a3[2 * n] = jnp.zeros((16, 128), BF16)

    def choose():
        await_bytes(a3.at[pl.ds(0, 2 * n - 2)], ar_rs.at[5])

        @pl.loop(0, n)
        def _(t):
            for g in range(fronts):
                c1[t, g] = a3[table[t * fronts + g]]

        @pl.loop(1, n)
        def _(i):
            peer = lax.rem(me + i, n)
            remote(
                c1.at[peer], c4.at[me // 2, c], ar_ss.at[6], ar_rs.at[6], {"blk": peer}
            ).start()

        c4[me // 2, c] = c1[me]

    def assemble():
        await_bytes(c1.at[pl.ds(0, n - 1)], ar_rs.at[6])
        for g in range(fronts):
            for h in range(2):
                big[g * size : g * size + size, 128 * h : 128 * h + 128] = c4[:, h, g].reshape(
                    size, 128
                )

    def chunk(owner):
        return dot(st_v[...], t_v[:, pl.ds(pl.multiple_of(owner * wide, 128), wide)])

    first, half, full = {}, {}, {}
    towards = (
        (lambda d: place(d, 0), lambda d: place(0, d)),
        (lambda d: place(0, d), lambda d: place(d, 0)),
    )

    def handle(h, d1, d2, v):
        go = towards[h][0]
        if d1 == 0:
            acc[h, d2] = v
            return
        if d1 == 2:
            slot, where = d2, go(1) if d2 < 2 else go(3)
        else:
            if (d2 < 2) == (d1 == 1):
                first[h, d2].wait_recv()
                v = v + s1_r[h, d2].astype(F32)
            slot, where = (4 + d2, go(1)) if d1 == 1 else (8 + d2, go(3))
        s1_s[h, slot] = v.astype(BF16)
        first[h, slot] = send(
            s1_s.at[h, slot], s1_r.at[h, slot], s1_ss.at[h, slot], s1_rs.at[h, slot], where
        )

    pairs = []

    def theirs(i):
        dx, dy = ORDER[i]
        pair_s[i] = chunk(chip(dx, dy) * 2 + (1 - c)).astype(BF16)
        pairs.append(send(pair_s.at[i], pair_r.at[i], pair_ss.at[i], pair_rs.at[i], partner))

    def ours(i):
        dx, dy = ORDER[i]
        v = chunk(chip(dx, dy) * 2 + c)
        pairs[i].wait_recv()
        v = v + pair_r[i].astype(F32)
        handle(0, dx, dy, v[:128])
        handle(1, dy, dx, v[128:])

    def second(d2, h):
        go = towards[h][1]
        first[h, 4 + d2].wait_recv()
        first[h, 8 + d2].wait_recv()
        v = acc[h, d2] + s1_r[h, 4 + d2].astype(F32) + s1_r[h, 8 + d2].astype(F32)
        if d2 == 2:
            for k in range(2):
                s2_s[h, k] = v[64 * k : 64 * k + 64].astype(BF16)
                half[h, k] = send(
                    s2_s.at[h, k], s2_r.at[h, k], s2_ss.at[h, k], s2_rs.at[h, k], go(1 + 2 * k)
                )
        elif d2 == 0:
            for k in range(2):
                full[h, k].wait_recv()
                v = v + s3_r[h, k].astype(F32)
            x_v[h * 128 : h * 128 + 128, :] = v
        else:
            k = d2 // 2
            half[h, k].wait_recv()
            more = s2_r[h, k].astype(F32)
            low, high = v[:64], v[64:]
            if k == 0:
                low = low + more
            else:
                high = high + more
            s3_s[h, k, 0:64, :] = low.astype(BF16)
            s3_s[h, k, 64:128, :] = high.astype(BF16)
            full[h, k] = send(s3_s.at[h, k], s3_r.at[h, k], s3_ss.at[h, k], s3_rs.at[h, k], go(d2))

    turn = (((1,), (1,)), ((), ()))
    z_sends = []

    def leave(h):
        low, up = 128 * h, 128 * h + 128
        lane = lax.broadcasted_iota(jnp.int32, (128, size), 1)
        line = lax.broadcasted_iota(jnp.int32, (128, size), 0) + low
        w_high, w_low = split(jnp.where(lane <= line, a_ref[low:up, :], 0.0))
        left = lax.dot_general(big[...], w_high, turn, preferred_element_type=F32)
        left = left + lax.dot_general(big[...], w_low, turn, preferred_element_type=F32)
        z_s[h] = left.astype(BF16).reshape(fronts, size, 128)
        for i in (2, 1, 3):
            g = lax.rem(front + i, fronts)
            z_sends.append(
                send(z_s.at[h, g], z_r.at[h, front], z_ss.at[h, i], z_rs.at[h, i], {"front": g})
            )
        z_r[h, front] = z_s[h, front]

    theirs(0)
    theirs(1)
    other.wait_recv()
    gm_mid[...] = (gm_send[c] + gm_pair[...]).astype(BF16)
    scatter(gm_mid, gm_recv, 2)
    spill()
    for i in range(2, 16):
        theirs(i)
        if 4 <= i < 8:
            ours(i - 4)
    all_came(gm_recv, 2)
    total = jnp.sum(gm_recv[...].astype(F32), axis=0)
    g_bc[...] = total[:8]
    m_bc[...] = total[8:]
    spread(g_bc, g_full, 3)
    for i in range(4, 11):
        ours(i)
    choose()
    second(2, 0)
    second(2, 1)
    for i in range(11, 16):
        ours(i)
    spread(m_bc, m_full, 4)
    join(g_full, 3, 3).wait_recv()
    a_ref[...] = g_full[...].reshape(size, size) * (1.0 / slab_rows)
    between = {
        64: lambda: (second(1, 0), second(1, 1)),
        128: lambda: (assemble(), leave(0)),
        192: lambda: (second(3, 0), second(3, 1)),
    }
    for count in factor_steps(a_ref):
        if count in between:
            between[count]()
    leave(1)
    join(m_full, 4, 4).wait_recv()
    mix_high, mix_low = split(m_full[...].reshape(size, size))
    prow = prow_ref[...]
    taken = dot(mix_high, prow) + dot(mix_low, prow)
    second(0, 0)
    second(0, 1)
    cross = x_v[...] - taken
    column = lax.broadcasted_iota(jnp.int32, (size, size), 1)
    w_high, w_low = split(jnp.where(column <= row, a_ref[...], 0.0))
    c_high, c_low = split(cross)
    right = dot(w_high, c_high) + dot(w_high, c_low) + dot(w_low, c_high)
    right_out[...] = (right.T * (1.0 / math.sqrt(slab_rows))).astype(BF16)
    for copy in z_sends:
        copy.wait_recv()
    z_out[...] = z_r[...]
    for copy in waits:
        copy.wait_send()
    await_bytes(q_mid.at[pl.ds(1, chips - 1)], ar_ss.at[0])
    await_bytes(q_mid.at[pl.ds(1, chips - 1)], ar_ss.at[1])
    await_bytes(gm_mid.at[pl.ds(1, chips - 1)], ar_ss.at[2])
    await_bytes(q_mid.at[pl.ds(1, chips - 1)], ar_ss.at[3])
    await_bytes(q_mid.at[pl.ds(1, chips - 1)], ar_ss.at[4])
    await_bytes(a3.at[pl.ds(0, 2 * n - 2)], ar_ss.at[5])
    await_bytes(c1.at[pl.ds(0, n - 1)], ar_ss.at[6])


def fused_call(slab_rows, table, column, inverse, rows, row_map, trailing, sketch):
    length, cols = trailing.shape
    wide = rows.shape[1]
    vmem = pl.BlockSpec(memory_space=pltpu.VMEM)
    anyw = pl.BlockSpec(memory_space=pl.ANY)
    dma = pltpu.SemaphoreType.DMA

    def kernel(*refs):
        fused_kernel(slab_rows, *refs)

    return pl.pallas_call(
        kernel,
        out_shape=(
            jax.ShapeDtypeStruct((length, 256), BF16),
            jax.ShapeDtypeStruct((wide, 256), BF16),
            jax.ShapeDtypeStruct((2, 4, 256, 128), BF16),
        ),
        in_specs=[pl.BlockSpec(memory_space=pltpu.SMEM), vmem, vmem, vmem, vmem, anyw, anyw],
        out_specs=(vmem, vmem, vmem),
        scratch_shapes=[
            pltpu.VMEM((length, cols), BF16),
            pltpu.VMEM((cols, 256), BF16),
            pltpu.VMEM((wide, 256), BF16),
            pltpu.VMEM((length, 256), F32),
            pltpu.VMEM((256, length), BF16),
            pltpu.VMEM((2, 16, 8, 256), F32),
            pltpu.VMEM((16, 8, 256), F32),
            pltpu.VMEM((16, 8, 256), F32),
            pltpu.VMEM((16, 8, 256), F32),
            pltpu.VMEM((8, 256), F32),
            pltpu.VMEM((2, 16, 8, 256), F32),
            pltpu.VMEM((2, 16, 16, 256), F32),
            pltpu.VMEM((16, 16, 256), F32),
            pltpu.VMEM((16, 16, 256), BF16),
            pltpu.VMEM((16, 16, 256), BF16),
            pltpu.VMEM((8, 256), F32),
            pltpu.VMEM((2, 16, 8, 256), F32),
            pltpu.VMEM((8, 256), F32),
            pltpu.VMEM((2, 16, 8, 256), F32),
            pltpu.VMEM((16, 256, wide), BF16),
            pltpu.VMEM((16, 256, wide), BF16),
            pltpu.VMEM((2, 12, 128, wide), BF16),
            pltpu.VMEM((2, 12, 128, wide), BF16),
            pltpu.VMEM((2, 4, 128, wide), F32),
            pltpu.VMEM((2, 2, 64, wide), BF16),
            pltpu.VMEM((2, 2, 64, wide), BF16),
            pltpu.VMEM((2, 2, 128, wide), BF16),
            pltpu.VMEM((2, 2, 128, wide), BF16),
            pltpu.VMEM((256, wide), F32),
            pltpu.VMEM((256, 256), F32),
            pltpu.VMEM((16, 2, 2, 16, 128), BF16),
            pltpu.VMEM((65, 16, 128), BF16),
            pltpu.VMEM((32, 4, 16, 128), BF16),
            pltpu.VMEM((16, 2, 4, 16, 128), BF16),
            pltpu.VMEM((1024, 256), BF16),
            pltpu.VMEM((2, 4, 256, 128), BF16),
            pltpu.VMEM((2, 4, 256, 128), BF16),
            dma((17,)),
            dma((7,)),
            dma((7,)),
            dma((5,)),
            dma((5,)),
            dma((16,)),
            dma((16,)),
            dma((2, 12)),
            dma((2, 12)),
            dma((2, 2)),
            dma((2, 2)),
            dma((2, 2)),
            dma((2, 2)),
            dma((2, 4)),
            dma((2, 4)),
        ],
        compiler_params=pltpu.CompilerParams(
            collective_id=0, has_side_effects=True, vmem_limit_bytes=VLIM
        ),
        name="fused",
    )(table, column, inverse, rows, row_map, trailing, sketch)


def write_kernel(l_ref, right_ref, z_ref, l_out, right_out, parent_out):
    l_out[...] = l_ref[...]
    right_out[...] = right_ref[...]
    for g in range(4):
        for h in range(2):
            at = g * 256 + 128 * h
            parent_out[:, at : at + 128] = z_ref[h, g]


def write_call(factored, right, parts):
    vmem = pl.BlockSpec(memory_space=pltpu.VMEM)
    return pl.pallas_call(
        write_kernel,
        out_shape=(
            jax.ShapeDtypeStruct(factored.shape, BF16),
            jax.ShapeDtypeStruct(right.shape, BF16),
            jax.ShapeDtypeStruct((256, 1024), BF16),
        ),
        in_specs=[vmem] * 3,
        out_specs=(vmem, vmem, vmem),
        name="write",
    )(factored, right, parts)


def slot_table(parent_block, parent_slot):
    front = lax.axis_index("front")
    blocks = lax.dynamic_slice(parent_block, (front, 0), (1, parent_block.shape[1]))[0]
    parents = jnp.arange(parent_slot.shape[0], dtype=jnp.int32)
    owners = jnp.sum(jnp.where(blocks[:, None] == parents[None, :], parent_slot[None, :], 0), axis=1)
    slot = jnp.arange(128, dtype=jnp.int32)
    device = slot % 4 * 32 + slot // 4
    j = jnp.arange(blocks.shape[0], dtype=jnp.int32)
    return 64 + jnp.sum(jnp.where(owners[None, :] == device[:, None], j[None, :] - 64, 0), axis=1)


def body(
    panel_column, upper_inverse, panel_rows, trailing, sketch, row_map, parent_block, parent_slot
):
    slab_rows = trailing.shape[1] * lax.axis_size("blk")
    results = fused_call(
        slab_rows,
        slot_table(parent_block, parent_slot),
        panel_column[0],
        upper_inverse[0],
        panel_rows[0],
        row_map[0],
        trailing[0],
        sketch,
    )
    factored, right, parent = write_call(*results)
    return factored[None], right[None], parent


def solution(mesh):
    return jax.shard_map(
        body,
        mesh=mesh,
        in_specs=(
            P("front", "blk", None),
            P("front", None, None),
            P("front", None, "blk"),
            P("front", "blk", None),
            P(),
            P("front", "blk", None),
            P(),
            P(),
        ),
        out_specs=(P("front", "blk", None), P("front", "blk", None), P(("front", "blk"), None)),
        check_vma=False,
    )
```

```python
import math

import jax
import jax.numpy as jnp
from jax import lax
from jax.experimental import pallas as pl
from jax.experimental.pallas import tpu as pltpu
from jax.sharding import PartitionSpec as P

F32 = jnp.float32
BF16 = jnp.bfloat16
MESH = pl.DeviceIdType.MESH
VLIM = 62 * 1024 * 1024

ORDER = (
    (2, 2), (2, 0), (0, 2), (2, 1), (1, 2), (2, 3), (3, 2), (1, 3),
    (3, 1), (3, 0), (0, 3), (1, 0), (0, 1), (1, 1), (3, 3), (0, 0),
)


def dot(a, b):
    return jnp.dot(a, b, preferred_element_type=F32)


def split(a):
    high = a.astype(BF16)
    return high, (a - high.astype(F32)).astype(BF16)


def remote(src, dst, send_sem, recv_sem, where):
    return pltpu.make_async_remote_copy(
        src_ref=src,
        dst_ref=dst,
        send_sem=send_sem,
        recv_sem=recv_sem,
        device_id=where,
        device_id_type=MESH,
    )


def await_bytes(ref, sem):
    pltpu.make_async_copy(ref, ref, sem).wait()


def as_column(line):
    k = line.shape[1]
    rows = lax.broadcasted_iota(jnp.int32, (k, k), 0)
    same = rows == lax.broadcasted_iota(jnp.int32, (k, k), 1)
    return jnp.sum(jnp.where(same, line, 0), axis=1, keepdims=True)


def slot_table(blocks, slots):
    count, parents = blocks.shape[1], slots.shape[1]
    number = lax.broadcasted_iota(jnp.int32, (parents, count), 0)
    hit = number == blocks
    owners = jnp.sum(jnp.where(hit, as_column(slots), 0), axis=0, keepdims=True)
    slot = lax.broadcasted_iota(jnp.int32, (count, 128), 1)
    device = slot % 4 * 32 + slot // 4
    j = lax.broadcasted_iota(jnp.int32, (count, 128), 0)
    goes = as_column(owners) == device
    return jnp.min(jnp.where(goes, j, count), axis=0, keepdims=True)


def factor_steps(a_ref, block=64, width=8, every=16):
    size = a_ref.shape[0]
    shape = (8, size)
    lane = lax.broadcasted_iota(jnp.int32, shape, 1)
    sub = lax.broadcasted_iota(jnp.int32, shape, 0)
    for k in range(size // block):
        base = k * block
        rest = base + block
        tiles = [a_ref[base + 8 * t : base + 8 * t + 8, :] for t in range(block // 8)]
        pivots = [jnp.ones(shape, F32) for _ in tiles]
        for j in range(0, block, width):
            at, low, own = base + j, j % 8, j // 8
            inside = (lane >= at) & (lane < at + width)

            def columns(tile):
                return [jnp.broadcast_to(tile[:, at + i : at + i + 1], shape) for i in range(width)]

            def line(tile, i):
                return jnp.broadcast_to(tile[low + i : low + i + 1, :], shape)

            mine = tiles[own]
            heads = columns(mine)
            m = [
                [line(heads[q], i) if q >= i else None for q in range(width)]
                for i in range(width)
            ]
            lines = [
                jnp.where(inside, jnp.where(lane == at + i, 1.0, 0.0), line(mine, i))
                for i in range(width)
            ]
            scales, mults = [], {}
            for i in range(width):
                inv = 1.0 / m[i][i]
                scales.append(inv)
                for q in range(i + 1, width):
                    mults[q, i] = m[i][q] * inv
                for q in range(i + 1, width):
                    for p in range(q, width):
                        m[q][p] = m[q][p] - mults[q, i] * m[i][p]
            for i in range(width):
                for q in range(i + 1, width):
                    lines[q] = lines[q] - mults[q, i] * lines[i]
            scaled = [lines[i] * scales[i] for i in range(width)]
            for t in range(own, block // 8):
                tile = tiles[t]
                cs = heads if t == own else columns(tile)
                cs = list(cs)
                for i in range(width):
                    for q in range(i + 1, width):
                        cs[q] = cs[q] - mults[q, i] * cs[i]
                out = jnp.where(inside, 0.0, tile)
                for i in range(width):
                    out = out - cs[i] * scaled[i]
                if t == own:
                    out = jnp.where(sub >= low + width, out, tile)
                    for i in range(width):
                        out = jnp.where(sub == low + i, lines[i], out)
                        pivots[t] = jnp.where(sub == low + i, m[i][i], pivots[t])
                tiles[t] = out
            if (j + width) % every == 0 and j + width < block:
                yield at + width
        for t in range(block // 8):
            stale = (lane > sub + (base + 8 * t)) & (lane < rest)
            tile = jnp.where(stale, 0.0, tiles[t] * lax.rsqrt(pivots[t]))
            a_ref[base + 8 * t : base + 8 * t + 8, :] = tile
        if rest < size:
            done = a_ref[base:rest, :]
            change = lax.dot_general(
                done[:, rest:],
                done,
                (((0,), (0,)), ((), ())),
                precision=lax.Precision.HIGHEST,
                preferred_element_type=F32,
            )
            column = lax.broadcasted_iota(jnp.int32, (size - rest, size), 1)
            within = (column >= base) & (column < rest)
            a_ref[rest:, :] = jnp.where(within, 0.0, a_ref[rest:, :]) - change
        yield rest


def fused_kernel(
    slab_rows,
    pb_ref, slot_ref, col_ref, uinv_ref, prow_ref, map_ref, t_hbm, om_hbm,
    l_out, right_out, z_out,
    t_v, om_v, own_v, y_v, st_v,
    q_send, q_pair, q_mid, q_recv, q_bc, q_full,
    gm_send, gm_pair, gm_mid, gm_recv, g_bc, g_full, m_bc, m_full,
    pair_s, pair_r, s1_s, s1_r, acc, s2_s, s2_r, s3_s, s3_r, x_v, a_ref,
    a0, a3, c1, c4, big, z_s, z_r,
    ld_sem, ar_ss, ar_rs, swap_ss, swap_rs, pair_ss, pair_rs, s1_ss, s1_rs, s2_ss, s2_rs, s3_ss, s3_rs,
    z_ss, z_rs, table_v, table, table_sem,
):
    me = lax.axis_index("blk")
    front = lax.axis_index("front")
    n, fronts, size = 32, 4, 256
    x, y, c = me // 8, (me // 2) % 4, me % 2
    cols = t_v.shape[1]
    wide = cols // n
    loads = 8
    step = cols // loads

    barrier = pltpu.get_barrier_semaphore()

    @pl.loop(1, n)
    def _(i):
        pl.semaphore_signal(
            barrier, inc=1, device_id={"blk": lax.rem(me + i, n)}, device_id_type=MESH
        )

    for i in range(1, fronts):
        pl.semaphore_signal(
            barrier, inc=1, device_id={"front": lax.rem(front + i, fronts)}, device_id_type=MESH
        )

    own_copy = pltpu.make_async_copy(
        om_hbm.at[pl.ds(pl.multiple_of(me * wide, wide), wide)], own_v, ld_sem.at[loads]
    )
    own_copy.start()
    copies = []
    for k in range(loads):
        part = pl.ds(k * step, step)
        pair = (
            pltpu.make_async_copy(om_hbm.at[part], om_v.at[part], ld_sem.at[loads + 1 + k]),
            pltpu.make_async_copy(t_hbm.at[:, part], t_v.at[:, part], ld_sem.at[k]),
        )
        for one in pair:
            one.start()
        copies.append(pair)

    chips = n // 2
    mine = me // 2

    def scatter(src, dst, phase):
        @pl.loop(1, chips)
        def _(i):
            peer = lax.rem(mine + i, chips)
            remote(
                src.at[peer], dst.at[i], ar_ss.at[phase], ar_rs.at[phase], {"blk": peer * 2 + c}
            ).start()

        dst[0] = src[mine]

    def spread(src, dst, phase):
        @pl.loop(1, chips)
        def _(i):
            peer = lax.rem(mine + i, chips)
            remote(
                src, dst.at[c, mine], ar_ss.at[phase], ar_rs.at[phase], {"blk": peer * 2 + c}
            ).start()

        dst[c, mine] = src[...]

    def all_came(dst, phase):
        await_bytes(dst.at[pl.ds(1, chips - 1)], ar_rs.at[phase])

    def swap(i, src, dst):
        return send(src, dst, swap_ss.at[i], swap_rs.at[i], partner)

    def join(full, phase, i):
        await_bytes(full.at[0, pl.ds(1, chips - 1)], ar_rs.at[phase])
        return swap(i, full.at[c], full.at[c])

    def chip(dx, dy):
        return lax.rem(x + dx, 4) * 4 + lax.rem(y + dy, 4)

    def place(dx, dy):
        return {"blk": chip(dx, dy) * 2 + c}

    partner = {"blk": chip(0, 0) * 2 + (1 - c)}
    waits = []

    def send(src, dst, ss, rs, where):
        copy = remote(src, dst, ss, rs, where)
        copy.start()
        waits.append(copy)
        return copy

    table_v[...] = slot_table(pb_ref[pl.ds(front, 1), :], slot_ref[...])
    table_copy = pltpu.make_async_copy(table_v, table, table_sem)
    table_copy.start()
    own_copy.wait()
    q_send[...] = dot(prow_ref[...], own_v[...]).reshape(q_send.shape)
    factored = dot(col_ref[...], uinv_ref[...]).astype(BF16)
    l_out[...] = factored
    pl.semaphore_wait(barrier, n - 1 + fronts - 1)
    other = swap(0, q_send.at[1 - c], q_pair)

    def sketch_step(k):
        for one in copies[k]:
            one.wait()
        part = pl.ds(k * step, step)
        out = dot(t_v[:, part], om_v[part, :])
        if k == 0:
            y_v[...] = out
        else:
            y_v[...] += out

    sketch_step(0)
    other.wait_recv()
    q_mid[...] = q_send[c] + q_pair[...]
    scatter(q_mid, q_recv, 0)
    for k in range(1, 4):
        sketch_step(k)
    all_came(q_recv, 0)
    q_bc[...] = jnp.sum(q_recv[...], axis=0)
    spread(q_bc, q_full, 1)
    for k in range(4, loads):
        sketch_step(k)
    join(q_full, 1, 1).wait_recv()
    q_high, q_low = split(q_full[...].reshape(size, size))
    sk32 = y_v[...] - dot(factored, q_high) - dot(factored, q_low)
    sk = sk32.astype(BF16)
    st_v[...] = sk32.T.astype(BF16)
    st = st_v[...]
    gm_send[:, :, :8, :] = dot(st, sk).reshape(2, chips, 8, size)
    gm_send[:, :, 8:, :] = dot(st, factored).reshape(2, chips, 8, size)
    other = swap(2, gm_send.at[1 - c], gm_pair)
    row = lax.broadcasted_iota(jnp.int32, (size, size), 0)
    for k in range(2):
        pick = (map_ref[k : k + 1, :] == row).astype(BF16)
        moved = dot(pick, sk[k * size : k * size + size]).astype(BF16)
        for h in range(2):
            a0[:, h, k] = moved[:, 128 * h : 128 * h + 128].reshape(16, 16, 128)

    def spill():
        @pl.loop(1, n)
        def _(i):
            peer = lax.rem(me + i, n)
            remote(
                a0.at[peer // 2, lax.rem(peer, 2)],
                a3.at[pl.ds(2 * me, 2)],
                ar_ss.at[5],
                ar_rs.at[5],
                {"blk": peer},
            ).start()

    a3[pl.ds(2 * me, 2)] = a0[me // 2, c]
    a3[2 * n] = jnp.zeros((16, 128), BF16)

    def choose():
        await_bytes(a3.at[pl.ds(0, 2 * n - 2)], ar_rs.at[5])
        table_copy.wait()

        @pl.loop(0, n)
        def _(t):
            for g in range(fronts):
                c1[t, g] = a3[table[0, t * fronts + g]]

        @pl.loop(1, n)
        def _(i):
            peer = lax.rem(me + i, n)
            remote(
                c1.at[peer], c4.at[me // 2, c], ar_ss.at[6], ar_rs.at[6], {"blk": peer}
            ).start()

        c4[me // 2, c] = c1[me]

    def assemble():
        await_bytes(c1.at[pl.ds(0, n - 1)], ar_rs.at[6])
        for g in range(fronts):
            for h in range(2):
                big[g * size : g * size + size, 128 * h : 128 * h + 128] = c4[:, h, g].reshape(
                    size, 128
                )

    def chunk(owner):
        return dot(st_v[...], t_v[:, pl.ds(pl.multiple_of(owner * wide, 128), wide)])

    first, half, full = {}, {}, {}
    towards = (
        (lambda d: place(d, 0), lambda d: place(0, d)),
        (lambda d: place(0, d), lambda d: place(d, 0)),
    )

    def handle(h, d1, d2, v):
        go = towards[h][0]
        if d1 == 0:
            acc[h, d2] = v
            return
        if d1 == 2:
            slot, where = d2, go(1) if d2 < 2 else go(3)
        else:
            if (d2 < 2) == (d1 == 1):
                first[h, d2].wait_recv()
                v = v + s1_r[h, d2].astype(F32)
            slot, where = (4 + d2, go(1)) if d1 == 1 else (8 + d2, go(3))
        s1_s[h, slot] = v.astype(BF16)
        first[h, slot] = send(
            s1_s.at[h, slot], s1_r.at[h, slot], s1_ss.at[h, slot], s1_rs.at[h, slot], where
        )

    pairs = []

    def theirs(i):
        dx, dy = ORDER[i]
        pair_s[i] = chunk(chip(dx, dy) * 2 + (1 - c)).astype(BF16)
        pairs.append(send(pair_s.at[i], pair_r.at[i], pair_ss.at[i], pair_rs.at[i], partner))

    def ours(i):
        dx, dy = ORDER[i]
        v = chunk(chip(dx, dy) * 2 + c)
        pairs[i].wait_recv()
        v = v + pair_r[i].astype(F32)
        handle(0, dx, dy, v[:128])
        handle(1, dy, dx, v[128:])

    def second(d2, h):
        go = towards[h][1]
        first[h, 4 + d2].wait_recv()
        first[h, 8 + d2].wait_recv()
        v = acc[h, d2] + s1_r[h, 4 + d2].astype(F32) + s1_r[h, 8 + d2].astype(F32)
        if d2 == 2:
            for k in range(2):
                s2_s[h, k] = v[64 * k : 64 * k + 64].astype(BF16)
                half[h, k] = send(
                    s2_s.at[h, k], s2_r.at[h, k], s2_ss.at[h, k], s2_rs.at[h, k], go(1 + 2 * k)
                )
        elif d2 == 0:
            for k in range(2):
                full[h, k].wait_recv()
                v = v + s3_r[h, k].astype(F32)
            x_v[h * 128 : h * 128 + 128, :] = v
        else:
            k = d2 // 2
            half[h, k].wait_recv()
            more = s2_r[h, k].astype(F32)
            low, high = v[:64], v[64:]
            if k == 0:
                low = low + more
            else:
                high = high + more
            s3_s[h, k, 0:64, :] = low.astype(BF16)
            s3_s[h, k, 64:128, :] = high.astype(BF16)
            full[h, k] = send(s3_s.at[h, k], s3_r.at[h, k], s3_ss.at[h, k], s3_rs.at[h, k], go(d2))

    turn = (((1,), (1,)), ((), ()))
    z_sends = []

    def leave(h):
        low, up = 128 * h, 128 * h + 128
        lane = lax.broadcasted_iota(jnp.int32, (128, size), 1)
        line = lax.broadcasted_iota(jnp.int32, (128, size), 0) + low
        w_high, w_low = split(jnp.where(lane <= line, a_ref[low:up, :], 0.0))
        left = lax.dot_general(big[...], w_high, turn, preferred_element_type=F32)
        left = left + lax.dot_general(big[...], w_low, turn, preferred_element_type=F32)
        z_s[h] = left.astype(BF16).reshape(fronts, size, 128)
        for i in (2, 1, 3):
            g = lax.rem(front + i, fronts)
            z_sends.append(
                send(z_s.at[h, g], z_r.at[h, front], z_ss.at[h, i], z_rs.at[h, i], {"front": g})
            )
        z_r[h, front] = z_s[h, front]

    theirs(0)
    theirs(1)
    other.wait_recv()
    gm_mid[...] = (gm_send[c] + gm_pair[...]).astype(BF16)
    scatter(gm_mid, gm_recv, 2)
    spill()
    for i in range(2, 16):
        theirs(i)
        if 4 <= i < 8:
            ours(i - 4)
    all_came(gm_recv, 2)
    total = jnp.sum(gm_recv[...].astype(F32), axis=0)
    g_bc[...] = total[:8]
    m_bc[...] = total[8:]
    spread(g_bc, g_full, 3)
    for i in range(4, 8):
        ours(i)
    choose()
    for i in range(8, 11):
        ours(i)
    second(2, 0)
    second(2, 1)
    for i in range(11, 16):
        ours(i)
    spread(m_bc, m_full, 4)
    join(g_full, 3, 3).wait_recv()
    a_ref[...] = g_full[...].reshape(size, size) * (1.0 / slab_rows)
    between = {
        64: lambda: (second(1, 0), second(1, 1)),
        128: lambda: (assemble(), leave(0)),
        192: lambda: (second(3, 0), second(3, 1)),
    }
    for count in factor_steps(a_ref):
        if count in between:
            between[count]()
    leave(1)
    join(m_full, 4, 4).wait_recv()
    mix_high, mix_low = split(m_full[...].reshape(size, size))
    prow = prow_ref[...]
    taken = dot(mix_high, prow) + dot(mix_low, prow)
    second(0, 0)
    second(0, 1)
    cross = x_v[...] - taken
    column = lax.broadcasted_iota(jnp.int32, (size, size), 1)
    w_high, w_low = split(jnp.where(column <= row, a_ref[...], 0.0))
    c_high, c_low = split(cross)
    right = dot(w_high, c_high) + dot(w_high, c_low) + dot(w_low, c_high)
    right_out[...] = (right.T * (1.0 / math.sqrt(slab_rows))).astype(BF16)
    for copy in z_sends:
        copy.wait_recv()
    z_out[...] = z_r[...]
    for copy in waits:
        copy.wait_send()
    await_bytes(q_mid.at[pl.ds(1, chips - 1)], ar_ss.at[0])
    await_bytes(q_mid.at[pl.ds(1, chips - 1)], ar_ss.at[1])
    await_bytes(gm_mid.at[pl.ds(1, chips - 1)], ar_ss.at[2])
    await_bytes(q_mid.at[pl.ds(1, chips - 1)], ar_ss.at[3])
    await_bytes(q_mid.at[pl.ds(1, chips - 1)], ar_ss.at[4])
    await_bytes(a3.at[pl.ds(0, 2 * n - 2)], ar_ss.at[5])
    await_bytes(c1.at[pl.ds(0, n - 1)], ar_ss.at[6])


def fused_call(slab_rows, blocks, slots, column, inverse, rows, row_map, trailing, sketch):
    length, cols = trailing.shape
    wide = rows.shape[1]
    vmem = pl.BlockSpec(memory_space=pltpu.VMEM)
    anyw = pl.BlockSpec(memory_space=pl.ANY)
    dma = pltpu.SemaphoreType.DMA

    def kernel(*refs):
        fused_kernel(slab_rows, *refs)

    return pl.pallas_call(
        kernel,
        out_shape=(
            jax.ShapeDtypeStruct((length, 256), BF16),
            jax.ShapeDtypeStruct((wide, 256), BF16),
            jax.ShapeDtypeStruct((2, 4, 256, 128), BF16),
        ),
        in_specs=[vmem] * 6 + [anyw, anyw],
        out_specs=(vmem, vmem, vmem),
        scratch_shapes=[
            pltpu.VMEM((length, cols), BF16),
            pltpu.VMEM((cols, 256), BF16),
            pltpu.VMEM((wide, 256), BF16),
            pltpu.VMEM((length, 256), F32),
            pltpu.VMEM((256, length), BF16),
            pltpu.VMEM((2, 16, 8, 256), F32),
            pltpu.VMEM((16, 8, 256), F32),
            pltpu.VMEM((16, 8, 256), F32),
            pltpu.VMEM((16, 8, 256), F32),
            pltpu.VMEM((8, 256), F32),
            pltpu.VMEM((2, 16, 8, 256), F32),
            pltpu.VMEM((2, 16, 16, 256), F32),
            pltpu.VMEM((16, 16, 256), F32),
            pltpu.VMEM((16, 16, 256), BF16),
            pltpu.VMEM((16, 16, 256), BF16),
            pltpu.VMEM((8, 256), F32),
            pltpu.VMEM((2, 16, 8, 256), F32),
            pltpu.VMEM((8, 256), F32),
            pltpu.VMEM((2, 16, 8, 256), F32),
            pltpu.VMEM((16, 256, wide), BF16),
            pltpu.VMEM((16, 256, wide), BF16),
            pltpu.VMEM((2, 12, 128, wide), BF16),
            pltpu.VMEM((2, 12, 128, wide), BF16),
            pltpu.VMEM((2, 4, 128, wide), F32),
            pltpu.VMEM((2, 2, 64, wide), BF16),
            pltpu.VMEM((2, 2, 64, wide), BF16),
            pltpu.VMEM((2, 2, 128, wide), BF16),
            pltpu.VMEM((2, 2, 128, wide), BF16),
            pltpu.VMEM((256, wide), F32),
            pltpu.VMEM((256, 256), F32),
            pltpu.VMEM((16, 2, 2, 16, 128), BF16),
            pltpu.VMEM((65, 16, 128), BF16),
            pltpu.VMEM((32, 4, 16, 128), BF16),
            pltpu.VMEM((16, 2, 4, 16, 128), BF16),
            pltpu.VMEM((1024, 256), BF16),
            pltpu.VMEM((2, 4, 256, 128), BF16),
            pltpu.VMEM((2, 4, 256, 128), BF16),
            dma((17,)),
            dma((7,)),
            dma((7,)),
            dma((5,)),
            dma((5,)),
            dma((16,)),
            dma((16,)),
            dma((2, 12)),
            dma((2, 12)),
            dma((2, 2)),
            dma((2, 2)),
            dma((2, 2)),
            dma((2, 2)),
            dma((2, 4)),
            dma((2, 4)),
            pltpu.VMEM((1, 128), jnp.int32),
            pltpu.SMEM((1, 128), jnp.int32),
            dma(()),
        ],
        compiler_params=pltpu.CompilerParams(
            collective_id=0, has_side_effects=True, vmem_limit_bytes=VLIM
        ),
        name="fused",
    )(blocks, slots, column, inverse, rows, row_map, trailing, sketch)


def write_kernel(l_ref, right_ref, z_ref, l_out, right_out, parent_out, l_v, right_v, z_v, in_sem, out_sem):
    routes = [(z_ref.at[h, g], z_v.at[h, g], (h, g)) for g in range(4) for h in range(2)]
    reads = [(z, v, parent_out.at[:, pl.ds(g * 256 + 128 * h, 128)]) for z, v, (h, g) in routes]
    reads += [(l_ref, l_v, l_out), (right_ref, right_v, right_out)]
    inward = [
        pltpu.make_async_copy(src, mid, in_sem.at[k]) for k, (src, mid, _) in enumerate(reads)
    ]
    outward = [
        pltpu.make_async_copy(mid, dst, out_sem.at[k]) for k, (_, mid, dst) in enumerate(reads)
    ]
    for copy in inward:
        copy.start()
    for came, copy in zip(inward, outward):
        came.wait()
        copy.start()
    for copy in outward:
        copy.wait()


def write_call(factored, right, parts):
    anyw = pl.BlockSpec(memory_space=pl.ANY)
    return pl.pallas_call(
        write_kernel,
        out_shape=(
            jax.ShapeDtypeStruct(factored.shape, BF16),
            jax.ShapeDtypeStruct(right.shape, BF16),
            jax.ShapeDtypeStruct((256, 1024), BF16),
        ),
        in_specs=[anyw] * 3,
        out_specs=(anyw, anyw, anyw),
        scratch_shapes=[
            pltpu.VMEM(factored.shape, BF16),
            pltpu.VMEM(right.shape, BF16),
            pltpu.VMEM(parts.shape, BF16),
            pltpu.SemaphoreType.DMA((10,)),
            pltpu.SemaphoreType.DMA((10,)),
        ],
        name="write",
    )(factored, right, parts)


def body(
    panel_column, upper_inverse, panel_rows, trailing, sketch, row_map, parent_block, parent_slot
):
    slab_rows = trailing.shape[1] * lax.axis_size("blk")
    results = fused_call(
        slab_rows,
        parent_block,
        parent_slot[None],
        panel_column[0],
        upper_inverse[0],
        panel_rows[0],
        row_map[0],
        trailing[0],
        sketch,
    )
    factored, right, parent = write_call(*results)
    return factored[None], right[None], parent


def solution(mesh):
    return jax.shard_map(
        body,
        mesh=mesh,
        in_specs=(
            P("front", "blk", None),
            P("front", None, None),
            P("front", None, "blk"),
            P("front", "blk", None),
            P(),
            P("front", "blk", None),
            P(),
            P(),
        ),
        out_specs=(P("front", "blk", None), P("front", "blk", None), P(("front", "blk"), None)),
        check_vma=False,
    )
```

```python
import math

import jax
import jax.numpy as jnp
from jax import lax
from jax.experimental import pallas as pl
from jax.experimental.pallas import tpu as pltpu
from jax.sharding import PartitionSpec as P

F32 = jnp.float32
BF16 = jnp.bfloat16
MESH = pl.DeviceIdType.MESH
VLIM = 62 * 1024 * 1024

ORDER = (
    (2, 2), (2, 0), (0, 2), (2, 1), (1, 2), (2, 3), (3, 2), (1, 3),
    (3, 1), (3, 0), (0, 3), (1, 0), (0, 1), (1, 1), (3, 3), (0, 0),
)


def dot(a, b):
    return jnp.dot(a, b, preferred_element_type=F32)


def split(a):
    high = a.astype(BF16)
    return high, (a - high.astype(F32)).astype(BF16)


def remote(src, dst, send_sem, recv_sem, where):
    return pltpu.make_async_remote_copy(
        src_ref=src,
        dst_ref=dst,
        send_sem=send_sem,
        recv_sem=recv_sem,
        device_id=where,
        device_id_type=MESH,
    )


def await_bytes(ref, sem):
    pltpu.make_async_copy(ref, ref, sem).wait()


def as_column(line):
    k = line.shape[1]
    rows = lax.broadcasted_iota(jnp.int32, (k, k), 0)
    same = rows == lax.broadcasted_iota(jnp.int32, (k, k), 1)
    return jnp.sum(jnp.where(same, line, 0), axis=1, keepdims=True)


def slot_table(blocks, slots):
    count, parents = blocks.shape[1], slots.shape[1]
    number = lax.broadcasted_iota(jnp.int32, (parents, count), 0)
    hit = number == blocks
    owners = jnp.sum(jnp.where(hit, as_column(slots), 0), axis=0, keepdims=True)
    slot = lax.broadcasted_iota(jnp.int32, (count, 128), 1)
    device = slot % 4 * 32 + slot // 4
    j = lax.broadcasted_iota(jnp.int32, (count, 128), 0)
    goes = as_column(owners) == device
    return jnp.min(jnp.where(goes, j, count), axis=0, keepdims=True)


def factor_steps(a_ref, block=64, width=8, every=16):
    size = a_ref.shape[0]
    shape = (8, size)
    lane = lax.broadcasted_iota(jnp.int32, shape, 1)
    sub = lax.broadcasted_iota(jnp.int32, shape, 0)
    for k in range(size // block):
        base = k * block
        rest = base + block
        tiles = [a_ref[base + 8 * t : base + 8 * t + 8, :] for t in range(block // 8)]
        pivots = [jnp.ones(shape, F32) for _ in tiles]
        for j in range(0, block, width):
            at, low, own = base + j, j % 8, j // 8
            inside = (lane >= at) & (lane < at + width)

            def columns(tile):
                return [jnp.broadcast_to(tile[:, at + i : at + i + 1], shape) for i in range(width)]

            def line(tile, i):
                return jnp.broadcast_to(tile[low + i : low + i + 1, :], shape)

            mine = tiles[own]
            heads = columns(mine)
            m = [
                [line(heads[q], i) if q >= i else None for q in range(width)]
                for i in range(width)
            ]
            lines = [
                jnp.where(inside, jnp.where(lane == at + i, 1.0, 0.0), line(mine, i))
                for i in range(width)
            ]
            scales, mults = [], {}
            for i in range(width):
                inv = 1.0 / m[i][i]
                scales.append(inv)
                for q in range(i + 1, width):
                    mults[q, i] = m[i][q] * inv
                for q in range(i + 1, width):
                    for p in range(q, width):
                        m[q][p] = m[q][p] - mults[q, i] * m[i][p]
            for i in range(width):
                for q in range(i + 1, width):
                    lines[q] = lines[q] - mults[q, i] * lines[i]
            scaled = [lines[i] * scales[i] for i in range(width)]
            for t in range(own, block // 8):
                tile = tiles[t]
                cs = heads if t == own else columns(tile)
                cs = list(cs)
                for i in range(width):
                    for q in range(i + 1, width):
                        cs[q] = cs[q] - mults[q, i] * cs[i]
                out = jnp.where(inside, 0.0, tile)
                for i in range(width):
                    out = out - cs[i] * scaled[i]
                if t == own:
                    out = jnp.where(sub >= low + width, out, tile)
                    for i in range(width):
                        out = jnp.where(sub == low + i, lines[i], out)
                        pivots[t] = jnp.where(sub == low + i, m[i][i], pivots[t])
                tiles[t] = out
            if (j + width) % every == 0 and j + width < block:
                yield at + width
        for t in range(block // 8):
            stale = (lane > sub + (base + 8 * t)) & (lane < rest)
            tile = jnp.where(stale, 0.0, tiles[t] * lax.rsqrt(pivots[t]))
            a_ref[base + 8 * t : base + 8 * t + 8, :] = tile
        if rest < size:
            done = a_ref[base:rest, :]
            change = lax.dot_general(
                done[:, rest:],
                done,
                (((0,), (0,)), ((), ())),
                precision=lax.Precision.HIGHEST,
                preferred_element_type=F32,
            )
            column = lax.broadcasted_iota(jnp.int32, (size - rest, size), 1)
            within = (column >= base) & (column < rest)
            a_ref[rest:, :] = jnp.where(within, 0.0, a_ref[rest:, :]) - change
        yield rest


def fused_kernel(
    slab_rows,
    pb_ref, slot_ref, col_ref, uinv_ref, prow_ref, map_ref, t_hbm, om_hbm,
    l_out, right_out, z_out,
    t_v, om_v, own_v, y_v, st_v,
    q_send, q_pair, q_mid, q_recv, q_bc, q_full,
    gm_send, gm_pair, gm_mid, gm_recv, g_bc, g_full, m_bc, m_full,
    pair_s, pair_r, s1_s, s1_r, acc, s2_s, s2_r, s3_s, s3_r, x_v, a_ref,
    a0, a3, c1, c4, big, z_s, z_r,
    ld_sem, ar_ss, ar_rs, swap_ss, swap_rs, pair_ss, pair_rs, s1_ss, s1_rs, s2_ss, s2_rs, s3_ss, s3_rs,
    z_ss, z_rs, table_v, table, table_sem,
):
    me = lax.axis_index("blk")
    front = lax.axis_index("front")
    n, fronts, size = 32, 4, 256
    x, y, c = me // 8, (me // 2) % 4, me % 2
    cols = t_v.shape[1]
    wide = cols // n
    loads = 8
    step = cols // loads

    barrier = pltpu.get_barrier_semaphore()

    @pl.loop(1, n)
    def _(i):
        pl.semaphore_signal(
            barrier, inc=1, device_id={"blk": lax.rem(me + i, n)}, device_id_type=MESH
        )

    for i in range(1, fronts):
        pl.semaphore_signal(
            barrier, inc=1, device_id={"front": lax.rem(front + i, fronts)}, device_id_type=MESH
        )

    own_copy = pltpu.make_async_copy(
        om_hbm.at[pl.ds(pl.multiple_of(me * wide, wide), wide)], own_v, ld_sem.at[loads]
    )
    own_copy.start()
    copies = []
    for k in range(loads):
        part = pl.ds(k * step, step)
        pair = (
            pltpu.make_async_copy(om_hbm.at[part], om_v.at[part], ld_sem.at[loads + 1 + k]),
            pltpu.make_async_copy(t_hbm.at[:, part], t_v.at[:, part], ld_sem.at[k]),
        )
        for one in pair:
            one.start()
        copies.append(pair)

    chips = n // 2
    mine = me // 2

    def scatter(src, dst, phase):
        @pl.loop(1, chips)
        def _(i):
            peer = lax.rem(mine + i, chips)
            remote(
                src.at[peer], dst.at[i], ar_ss.at[phase], ar_rs.at[phase], {"blk": peer * 2 + c}
            ).start()

        dst[0] = src[mine]

    def spread(src, dst, phase):
        @pl.loop(1, chips)
        def _(i):
            peer = lax.rem(mine + i, chips)
            remote(
                src, dst.at[c, mine], ar_ss.at[phase], ar_rs.at[phase], {"blk": peer * 2 + c}
            ).start()

        dst[c, mine] = src[...]

    def all_came(dst, phase):
        await_bytes(dst.at[pl.ds(1, chips - 1)], ar_rs.at[phase])

    def swap(i, src, dst):
        return send(src, dst, swap_ss.at[i], swap_rs.at[i], partner)

    def join(full, phase, i):
        await_bytes(full.at[0, pl.ds(1, chips - 1)], ar_rs.at[phase])
        return swap(i, full.at[c], full.at[c])

    def chip(dx, dy):
        return lax.rem(x + dx, 4) * 4 + lax.rem(y + dy, 4)

    def place(dx, dy):
        return {"blk": chip(dx, dy) * 2 + c}

    partner = {"blk": chip(0, 0) * 2 + (1 - c)}
    waits = []

    def send(src, dst, ss, rs, where):
        copy = remote(src, dst, ss, rs, where)
        copy.start()
        waits.append(copy)
        return copy

    table_v[...] = slot_table(pb_ref[pl.ds(front, 1), :], slot_ref[...])
    table_copy = pltpu.make_async_copy(table_v, table, table_sem)
    table_copy.start()
    own_copy.wait()
    q_send[...] = dot(prow_ref[...], own_v[...]).reshape(q_send.shape)
    factored = dot(col_ref[...], uinv_ref[...]).astype(BF16)
    l_out[...] = factored
    pl.semaphore_wait(barrier, n - 1 + fronts - 1)
    other = swap(0, q_send.at[1 - c], q_pair)

    def sketch_step(k):
        for one in copies[k]:
            one.wait()
        part = pl.ds(k * step, step)
        out = dot(t_v[:, part], om_v[part, :])
        if k == 0:
            y_v[...] = out
        else:
            y_v[...] += out

    sketch_step(0)
    other.wait_recv()
    q_mid[...] = q_send[c] + q_pair[...]
    scatter(q_mid, q_recv, 0)
    for k in range(1, 4):
        sketch_step(k)
    all_came(q_recv, 0)
    q_bc[...] = jnp.sum(q_recv[...], axis=0)
    spread(q_bc, q_full, 1)
    for k in range(4, loads):
        sketch_step(k)
    join(q_full, 1, 1).wait_recv()
    q_high, q_low = split(q_full[...].reshape(size, size))
    sk32 = y_v[...] - dot(factored, q_high) - dot(factored, q_low)
    sk = sk32.astype(BF16)
    st_v[...] = sk32.T.astype(BF16)
    st = st_v[...]
    gm_send[:, :, :8, :] = dot(st, sk).reshape(2, chips, 8, size)
    gm_send[:, :, 8:, :] = dot(st, factored).reshape(2, chips, 8, size)
    other = swap(2, gm_send.at[1 - c], gm_pair)
    row = lax.broadcasted_iota(jnp.int32, (size, size), 0)
    for k in range(2):
        pick = (map_ref[k : k + 1, :] == row).astype(BF16)
        moved = dot(pick, sk[k * size : k * size + size]).astype(BF16)
        for h in range(2):
            a0[:, h, k] = moved[:, 128 * h : 128 * h + 128].reshape(16, 16, 128)

    def spill():
        @pl.loop(1, n)
        def _(i):
            peer = lax.rem(me + i, n)
            remote(
                a0.at[peer // 2, lax.rem(peer, 2)],
                a3.at[pl.ds(2 * me, 2)],
                ar_ss.at[5],
                ar_rs.at[5],
                {"blk": peer},
            ).start()

    a3[pl.ds(2 * me, 2)] = a0[me // 2, c]
    a3[2 * n] = jnp.zeros((16, 128), BF16)

    def choose():
        await_bytes(a3.at[pl.ds(0, 2 * n - 2)], ar_rs.at[5])
        table_copy.wait()

        @pl.loop(0, n)
        def _(t):
            for g in range(fronts):
                c1[t, g] = a3[table[0, t * fronts + g]]

        @pl.loop(1, n)
        def _(i):
            peer = lax.rem(me + i, n)
            remote(
                c1.at[peer], c4.at[me // 2, c], ar_ss.at[6], ar_rs.at[6], {"blk": peer}
            ).start()

        c4[me // 2, c] = c1[me]

    def assemble():
        await_bytes(c1.at[pl.ds(0, n - 1)], ar_rs.at[6])
        for g in range(fronts):
            for h in range(2):
                big[g * size : g * size + size, 128 * h : 128 * h + 128] = c4[:, h, g].reshape(
                    size, 128
                )

    def chunk(owner):
        return dot(st_v[...], t_v[:, pl.ds(pl.multiple_of(owner * wide, 128), wide)])

    first, half, full = {}, {}, {}
    towards = (
        (lambda d: place(d, 0), lambda d: place(0, d)),
        (lambda d: place(0, d), lambda d: place(d, 0)),
    )

    def handle(h, d1, d2, v):
        go = towards[h][0]
        if d1 == 0:
            acc[h, d2] = v
            return
        if d1 == 2:
            slot, where = d2, go(1) if d2 < 2 else go(3)
        else:
            if (d2 < 2) == (d1 == 1):
                first[h, d2].wait_recv()
                v = v + s1_r[h, d2].astype(F32)
            slot, where = (4 + d2, go(1)) if d1 == 1 else (8 + d2, go(3))
        s1_s[h, slot] = v.astype(BF16)
        first[h, slot] = send(
            s1_s.at[h, slot], s1_r.at[h, slot], s1_ss.at[h, slot], s1_rs.at[h, slot], where
        )

    pairs = []

    def theirs(i):
        dx, dy = ORDER[i]
        pair_s[i] = chunk(chip(dx, dy) * 2 + (1 - c)).astype(BF16)
        pairs.append(send(pair_s.at[i], pair_r.at[i], pair_ss.at[i], pair_rs.at[i], partner))

    def ours(i):
        dx, dy = ORDER[i]
        v = chunk(chip(dx, dy) * 2 + c)
        pairs[i].wait_recv()
        v = v + pair_r[i].astype(F32)
        handle(0, dx, dy, v[:128])
        handle(1, dy, dx, v[128:])

    def second(d2, h):
        go = towards[h][1]
        first[h, 4 + d2].wait_recv()
        first[h, 8 + d2].wait_recv()
        v = acc[h, d2] + s1_r[h, 4 + d2].astype(F32) + s1_r[h, 8 + d2].astype(F32)
        if d2 == 2:
            for k in range(2):
                s2_s[h, k] = v[64 * k : 64 * k + 64].astype(BF16)
                half[h, k] = send(
                    s2_s.at[h, k], s2_r.at[h, k], s2_ss.at[h, k], s2_rs.at[h, k], go(1 + 2 * k)
                )
        elif d2 == 0:
            for k in range(2):
                full[h, k].wait_recv()
                v = v + s3_r[h, k].astype(F32)
            x_v[h * 128 : h * 128 + 128, :] = v
        else:
            k = d2 // 2
            half[h, k].wait_recv()
            more = s2_r[h, k].astype(F32)
            low, high = v[:64], v[64:]
            if k == 0:
                low = low + more
            else:
                high = high + more
            s3_s[h, k, 0:64, :] = low.astype(BF16)
            s3_s[h, k, 64:128, :] = high.astype(BF16)
            full[h, k] = send(s3_s.at[h, k], s3_r.at[h, k], s3_ss.at[h, k], s3_rs.at[h, k], go(d2))

    turn = (((1,), (1,)), ((), ()))
    z_sends = []

    def leave(h):
        low, up = 128 * h, 128 * h + 128
        lane = lax.broadcasted_iota(jnp.int32, (128, size), 1)
        line = lax.broadcasted_iota(jnp.int32, (128, size), 0) + low
        w_high, w_low = split(jnp.where(lane <= line, a_ref[low:up, :], 0.0))
        left = lax.dot_general(big[...], w_high, turn, preferred_element_type=F32)
        left = left + lax.dot_general(big[...], w_low, turn, preferred_element_type=F32)
        z_s[h] = left.astype(BF16).reshape(fronts, size, 128)
        for i in (2, 1, 3):
            g = lax.rem(front + i, fronts)
            z_sends.append(
                send(z_s.at[h, g], z_r.at[h, front], z_ss.at[h, i], z_rs.at[h, i], {"front": g})
            )
        z_r[h, front] = z_s[h, front]

    theirs(0)
    theirs(1)
    other.wait_recv()
    gm_mid[...] = (gm_send[c] + gm_pair[...]).astype(BF16)
    scatter(gm_mid, gm_recv, 2)
    spill()
    for i in range(2, 16):
        theirs(i)
        if 4 <= i < 8:
            ours(i - 4)
    all_came(gm_recv, 2)
    total = jnp.sum(gm_recv[...].astype(F32), axis=0)
    g_bc[...] = total[:8]
    m_bc[...] = total[8:]
    spread(g_bc, g_full, 3)
    for i in range(4, 8):
        ours(i)
    choose()
    for i in range(8, 11):
        ours(i)
    second(2, 0)
    second(2, 1)
    for i in range(11, 16):
        ours(i)
    spread(m_bc, m_full, 4)
    join(g_full, 3, 3).wait_recv()
    a_ref[...] = g_full[...].reshape(size, size) * (1.0 / slab_rows)
    between = {
        64: lambda: (second(1, 0), second(1, 1)),
        128: lambda: (assemble(), leave(0)),
        192: lambda: (second(3, 0), second(3, 1), joins.append(join(m_full, 4, 4))),
    }
    joins = []
    for count in factor_steps(a_ref):
        if count in between:
            between[count]()
    leave(1)
    joins[0].wait_recv()
    mix_high, mix_low = split(m_full[...].reshape(size, size))
    prow = prow_ref[...]
    taken = dot(mix_high, prow) + dot(mix_low, prow)
    for copy in z_sends[:3]:
        copy.wait_recv()
    z_out[0] = z_r[0]
    second(0, 0)
    second(0, 1)
    cross = x_v[...] - taken
    column = lax.broadcasted_iota(jnp.int32, (size, size), 1)
    w_high, w_low = split(jnp.where(column <= row, a_ref[...], 0.0))
    c_high, c_low = split(cross)
    right = dot(w_high, c_high) + dot(w_high, c_low) + dot(w_low, c_high)
    right_out[...] = (right.T * (1.0 / math.sqrt(slab_rows))).astype(BF16)
    for copy in z_sends[3:]:
        copy.wait_recv()
    z_out[1] = z_r[1]
    for copy in waits:
        copy.wait_send()
    await_bytes(q_mid.at[pl.ds(1, chips - 1)], ar_ss.at[0])
    await_bytes(q_mid.at[pl.ds(1, chips - 1)], ar_ss.at[1])
    await_bytes(gm_mid.at[pl.ds(1, chips - 1)], ar_ss.at[2])
    await_bytes(q_mid.at[pl.ds(1, chips - 1)], ar_ss.at[3])
    await_bytes(q_mid.at[pl.ds(1, chips - 1)], ar_ss.at[4])
    await_bytes(a3.at[pl.ds(0, 2 * n - 2)], ar_ss.at[5])
    await_bytes(c1.at[pl.ds(0, n - 1)], ar_ss.at[6])


def fused_call(slab_rows, blocks, slots, column, inverse, rows, row_map, trailing, sketch):
    length, cols = trailing.shape
    wide = rows.shape[1]
    vmem = pl.BlockSpec(memory_space=pltpu.VMEM)
    anyw = pl.BlockSpec(memory_space=pl.ANY)
    dma = pltpu.SemaphoreType.DMA

    def kernel(*refs):
        fused_kernel(slab_rows, *refs)

    return pl.pallas_call(
        kernel,
        out_shape=(
            jax.ShapeDtypeStruct((length, 256), BF16),
            jax.ShapeDtypeStruct((wide, 256), BF16),
            jax.ShapeDtypeStruct((2, 4, 256, 128), BF16),
        ),
        in_specs=[vmem] * 6 + [anyw, anyw],
        out_specs=(vmem, vmem, vmem),
        scratch_shapes=[
            pltpu.VMEM((length, cols), BF16),
            pltpu.VMEM((cols, 256), BF16),
            pltpu.VMEM((wide, 256), BF16),
            pltpu.VMEM((length, 256), F32),
            pltpu.VMEM((256, length), BF16),
            pltpu.VMEM((2, 16, 8, 256), F32),
            pltpu.VMEM((16, 8, 256), F32),
            pltpu.VMEM((16, 8, 256), F32),
            pltpu.VMEM((16, 8, 256), F32),
            pltpu.VMEM((8, 256), F32),
            pltpu.VMEM((2, 16, 8, 256), F32),
            pltpu.VMEM((2, 16, 16, 256), F32),
            pltpu.VMEM((16, 16, 256), F32),
            pltpu.VMEM((16, 16, 256), BF16),
            pltpu.VMEM((16, 16, 256), BF16),
            pltpu.VMEM((8, 256), F32),
            pltpu.VMEM((2, 16, 8, 256), F32),
            pltpu.VMEM((8, 256), F32),
            pltpu.VMEM((2, 16, 8, 256), F32),
            pltpu.VMEM((16, 256, wide), BF16),
            pltpu.VMEM((16, 256, wide), BF16),
            pltpu.VMEM((2, 12, 128, wide), BF16),
            pltpu.VMEM((2, 12, 128, wide), BF16),
            pltpu.VMEM((2, 4, 128, wide), F32),
            pltpu.VMEM((2, 2, 64, wide), BF16),
            pltpu.VMEM((2, 2, 64, wide), BF16),
            pltpu.VMEM((2, 2, 128, wide), BF16),
            pltpu.VMEM((2, 2, 128, wide), BF16),
            pltpu.VMEM((256, wide), F32),
            pltpu.VMEM((256, 256), F32),
            pltpu.VMEM((16, 2, 2, 16, 128), BF16),
            pltpu.VMEM((65, 16, 128), BF16),
            pltpu.VMEM((32, 4, 16, 128), BF16),
            pltpu.VMEM((16, 2, 4, 16, 128), BF16),
            pltpu.VMEM((1024, 256), BF16),
            pltpu.VMEM((2, 4, 256, 128), BF16),
            pltpu.VMEM((2, 4, 256, 128), BF16),
            dma((17,)),
            dma((7,)),
            dma((7,)),
            dma((5,)),
            dma((5,)),
            dma((16,)),
            dma((16,)),
            dma((2, 12)),
            dma((2, 12)),
            dma((2, 2)),
            dma((2, 2)),
            dma((2, 2)),
            dma((2, 2)),
            dma((2, 4)),
            dma((2, 4)),
            pltpu.VMEM((1, 128), jnp.int32),
            pltpu.SMEM((1, 128), jnp.int32),
            dma(()),
        ],
        compiler_params=pltpu.CompilerParams(
            collective_id=0, has_side_effects=True, vmem_limit_bytes=VLIM
        ),
        name="fused",
    )(blocks, slots, column, inverse, rows, row_map, trailing, sketch)


def write_kernel(l_ref, right_ref, z_ref, l_out, right_out, parent_out, l_v, right_v, z_v, in_sem, out_sem):
    routes = [(z_ref.at[h, g], z_v.at[h, g], (h, g)) for g in range(4) for h in range(2)]
    reads = [(z, v, parent_out.at[:, pl.ds(g * 256 + 128 * h, 128)]) for z, v, (h, g) in routes]
    reads += [(l_ref, l_v, l_out), (right_ref, right_v, right_out)]
    inward = [
        pltpu.make_async_copy(src, mid, in_sem.at[k]) for k, (src, mid, _) in enumerate(reads)
    ]
    outward = [
        pltpu.make_async_copy(mid, dst, out_sem.at[k]) for k, (_, mid, dst) in enumerate(reads)
    ]
    for copy in inward:
        copy.start()
    for came, copy in zip(inward, outward):
        came.wait()
        copy.start()
    for copy in outward:
        copy.wait()


def write_call(factored, right, parts):
    anyw = pl.BlockSpec(memory_space=pl.ANY)
    return pl.pallas_call(
        write_kernel,
        out_shape=(
            jax.ShapeDtypeStruct(factored.shape, BF16),
            jax.ShapeDtypeStruct(right.shape, BF16),
            jax.ShapeDtypeStruct((256, 1024), BF16),
        ),
        in_specs=[anyw] * 3,
        out_specs=(anyw, anyw, anyw),
        scratch_shapes=[
            pltpu.VMEM(factored.shape, BF16),
            pltpu.VMEM(right.shape, BF16),
            pltpu.VMEM(parts.shape, BF16),
            pltpu.SemaphoreType.DMA((10,)),
            pltpu.SemaphoreType.DMA((10,)),
        ],
        name="write",
    )(factored, right, parts)


def body(
    panel_column, upper_inverse, panel_rows, trailing, sketch, row_map, parent_block, parent_slot
):
    slab_rows = trailing.shape[1] * lax.axis_size("blk")
    results = fused_call(
        slab_rows,
        parent_block,
        parent_slot[None],
        panel_column[0],
        upper_inverse[0],
        panel_rows[0],
        row_map[0],
        trailing[0],
        sketch,
    )
    factored, right, parent = write_call(*results)
    return factored[None], right[None], parent


def solution(mesh):
    return jax.shard_map(
        body,
        mesh=mesh,
        in_specs=(
            P("front", "blk", None),
            P("front", None, None),
            P("front", None, "blk"),
            P("front", "blk", None),
            P(),
            P("front", "blk", None),
            P(),
            P(),
        ),
        out_specs=(P("front", "blk", None), P("front", "blk", None), P(("front", "blk"), None)),
        check_vma=False,
    )
```
